256 devices in a mesh: ctx: 64 (over z, y, x_hi), head: 4 (over x_lo, core).
Axes of the slice: x: 4 (x_hi: 2, x_lo: 2; x = x_hi * 2 + x_lo), y: 4, z: 8, core: 2. Of those that a mesh axis runs over, the one named last changes fastest.
Arguments:
- prompt_keys: bfloat16 [16384, 8, 128], P('ctx', 'head'), may hold values from -12 to 12
- prompt_values: bfloat16 [16384, 8, 128], P('ctx', 'head'), may hold values from -6 to 6
- prompt_mask: int32 [16384], P('ctx'), may hold values from 0 to 1
- response_queries: bfloat16 [512, 2, 40, 128], P(('ctx', 'head')), may hold values from -16 to 16
- response_keys: bfloat16 [512, 2, 8, 128], P(('ctx', 'head')), may hold values from -8 to 8
- response_values: bfloat16 [512, 2, 8, 128], P(('ctx', 'head')), may hold values from -6 to 6
- resp_lengths: int32 [2], replicated, may hold values from 256 to 512
- prompt_reach: int32 [2], replicated, may hold values from 8192 to 16384
Outputs:
- attended: bfloat16 [512, 2, 40, 128], P(('ctx', 'head'))
The draws below stay inside these ranges and needn't reach their ends.
All inputs are finite; a program needn't handle non-finite values.
Results may differ from the reference program's by a relative error of at most 0.0031.
Values may be sent and summed in bfloat16 or wider, within the bound.
No kernel may reach another device: no remote copies, remote signals or barrier semaphores. Data moves between devices by JAX's collectives and lax.ppermute only.
A program may use at most 64 MiB of HBM per device.

```python
import math
import jax
import jax.numpy as jnp
from jax import lax

H = 40
KV = 8
HD = 128
RESP = 512
PROMPT_DEV = 256
PROMPT = 16384


def sign_table(key):
    drawn_picks = jax.random.randint(jax.random.fold_in(key, 202), (KV, HD), 0, 2)
    return jnp.where(drawn_picks == 1, 1.0, -1.0).astype(jnp.float32)


def drawn_place(key):
    return jax.random.randint(jax.random.fold_in(key, 101), (), 0, PROMPT // 2 - 1).astype(jnp.int32)


def draw_prompt_keys(key, part):
    scale_key = jax.random.fold_in(key, 11)
    noise_key = jax.random.fold_in(key, 12)
    scales = jnp.exp(jax.random.uniform(scale_key, (PROMPT, 1, 1), minval=math.log(0.7), maxval=math.log(1.4)))
    key_values = scales * jax.random.normal(noise_key, (PROMPT, KV, HD))
    return jnp.clip(key_values, -12.0, 12.0).astype(jnp.bfloat16)


def draw_response_queries(key, part):
    noise_key = jax.random.fold_in(key, 22)
    lead_rows = jnp.repeat(sign_table(key), H // KV, axis=0)
    query_values = 3.0 * jax.random.normal(noise_key, (RESP, 2, H, HD)) + 0.5 * lead_rows[None, None]
    return jnp.clip(query_values, -16.0, 16.0).astype(jnp.bfloat16)


def draw_response_keys(key, part):
    noise_key = jax.random.fold_in(key, 31)
    sign_rows = sign_table(key)
    noise_values = jax.random.normal(noise_key, (RESP, 2, KV, HD))
    return jnp.clip(noise_values + 0.5 * sign_rows[None, None], -8.0, 8.0).astype(jnp.bfloat16)


def draw_prompt_mask(key, part):
    drawn_picks = jax.random.randint(jax.random.fold_in(key, 41), (PROMPT,), 0, 8)
    mask_values = (drawn_picks > 0).astype(jnp.int32)
    planted = drawn_place(key)
    positions = jnp.arange(PROMPT, dtype=jnp.int32)
    return jnp.where((positions == planted) | (positions == planted + 1), 1, mask_values).astype(jnp.int32)


def draw_resp_lengths(key, part):
    second = jax.random.randint(jax.random.fold_in(key, 51), (1,), RESP // 2, RESP + 1)
    return jnp.concatenate([jnp.full((1,), RESP, jnp.int32), second.astype(jnp.int32)])


def draw_prompt_reach(key, part):
    second = jax.random.randint(jax.random.fold_in(key, 61), (1,), PROMPT // 2, PROMPT + 1)
    return jnp.concatenate([jnp.full((1,), PROMPT, jnp.int32), second.astype(jnp.int32)])


def steps_of(own_key, extent, cuts, smallest, high):
    level = 1.0
    for dim, blocks in cuts:
        steps = jax.random.uniform(jax.random.fold_in(jax.random.fold_in(own_key, 6), dim), (blocks,), jnp.float32, smallest / len(cuts), high / len(cuts))
        level = level * jnp.repeat(jnp.exp(steps), extent[dim] // blocks).reshape((-1,) + (1,) * (len(extent) - 1 - dim))
    return level


def normal_values(rng, shape, scale, bound, shards=(), held_as=jnp.bfloat16):
    loudness = steps_of(rng, shape, shards, -0.22, 0.18) if shards else 1.0
    drawn = jax.random.normal(rng, shape, jnp.float32) * scale * loudness
    return jnp.minimum(jnp.maximum(drawn, -bound), bound).astype(held_as)


def setup_inputs(seed: int = 0) -> dict:
    key_list = jax.random.split(jax.random.key(seed), 9)
    return {
        "prompt_keys": draw_prompt_keys(jax.random.fold_in(key_list[8], 71), 0),
        "prompt_values": normal_values(key_list[1], (PROMPT, KV, HD), 1.0, 6.0, ((0, 64), (1, 4))),
        "prompt_mask": draw_prompt_mask(jax.random.fold_in(key_list[8], 71), 0),
        "response_queries": draw_response_queries(jax.random.fold_in(key_list[8], 71), 0),
        "response_keys": draw_response_keys(jax.random.fold_in(key_list[8], 71), 0),
        "response_values": normal_values(key_list[5], (RESP, 2, KV, HD), 1.0, 6.0, ((0, 256),)),
        "resp_lengths": draw_resp_lengths(jax.random.fold_in(key_list[8], 71), 0),
        "prompt_reach": draw_prompt_reach(jax.random.fold_in(key_list[8], 71), 0),
    }


lowest = -1e+30

def reference(prompt_keys, prompt_values, prompt_mask, response_queries, response_keys, response_values, resp_lengths, prompt_reach):
    group_size = H // KV
    score_scale = 1.0 / math.sqrt(HD)
    queries = response_queries.astype(jnp.float32).reshape(RESP, 2, KV, group_size, HD)
    own_keys = response_keys.astype(jnp.float32)
    own_values = response_values.astype(jnp.float32)
    row_places = jnp.arange(RESP, dtype=jnp.int32)
    own_seen = row_places[None, :] <= row_places[:, None]
    own_scores = jnp.einsum('trgjd,srgd->trgjs', queries, own_keys) * score_scale
    own_scores = jnp.where(own_seen[:, None, None, None, :], own_scores, lowest)
    block_count = PROMPT // PROMPT_DEV

    def block_scores(block_index):
        first_place = block_index * PROMPT_DEV
        key_part = lax.dynamic_slice_in_dim(prompt_keys, first_place, PROMPT_DEV, 0).astype(jnp.float32)
        mask_part = lax.dynamic_slice_in_dim(prompt_mask, first_place, PROMPT_DEV, 0)
        scores = jnp.einsum('trgjd,pgd->trgjp', queries, key_part) * score_scale
        key_places = first_place + jnp.arange(PROMPT_DEV, dtype=jnp.int32)
        visible = (mask_part[None, :] == 1) & (key_places[None, :] < prompt_reach[:, None])
        return jnp.where(visible[None, :, None, None, :], scores, lowest)
    block_tops = lax.map(lambda block_index: lax.optimization_barrier(jnp.max(block_scores(block_index), axis=-1)), jnp.arange(block_count, dtype=jnp.int32))
    row_tops = jnp.maximum(lax.optimization_barrier(jnp.max(block_tops, axis=0)), lax.optimization_barrier(jnp.max(own_scores, axis=-1)))

    def visit_block(running, block_index):
        weights = jnp.exp(block_scores(block_index) - row_tops[..., None])
        value_part = lax.dynamic_slice_in_dim(prompt_values, block_index * PROMPT_DEV, PROMPT_DEV, 0).astype(jnp.float32)
        rounded = weights.astype(jnp.bfloat16).astype(jnp.float32)
        more_sums = jnp.einsum('trgjp,pgd->trgjd', rounded, value_part)
        return ((running[0] + lax.optimization_barrier(jnp.sum(weights, axis=-1)), running[1] + more_sums), None)
    initial = (jnp.zeros(row_tops.shape, jnp.float32), jnp.zeros(queries.shape, jnp.float32))
    (totals, summed), unused = lax.scan(visit_block, initial, jnp.arange(block_count, dtype=jnp.int32))
    own_weights = jnp.exp(own_scores - row_tops[..., None])
    own_rounded = own_weights.astype(jnp.bfloat16).astype(jnp.float32)
    totals = totals + lax.optimization_barrier(jnp.sum(own_weights, axis=-1))
    summed = summed + jnp.einsum('trgjs,srgd->trgjd', own_rounded, own_values)
    live_rows = row_places[:, None] < resp_lengths[None, :]
    attended = jnp.where(live_rows[:, :, None, None, None], summed / totals[..., None], 0.0)
    return attended.reshape(RESP, 2, H, HD).astype(jnp.bfloat16)
```

```python
import functools
import math

import jax
import jax.numpy as jnp
from jax import lax
from jax.experimental import pallas as pl
from jax.experimental.pallas import tpu as pltpu
from jax.sharding import Mesh, PartitionSpec as P

Z, Y, XH, XL, C = 8, 4, 2, 2, 2
PLANE = Y * XH * XL * C
HOLD = Y * XH
T, R, G, J, D = 2, 2, 2, 5, 128
LIVE = R * T * J
ROWS = 24
OWN = Z * PLANE
PROMPT_DEV = 256
LOWEST = -1e30
LOG2E = math.log2(math.e)
F32 = jnp.float32
BF16 = jnp.bfloat16


def three_parts(x):
    hi = x.astype(BF16).astype(F32)
    mid = (x - hi).astype(BF16).astype(F32)
    lo = (x - hi - mid).astype(BF16).astype(F32)
    return hi, mid, lo


def attend_kernel(info_ref, q_ref, kv_ref, own_ref, out_ref, bias_ref):
    z = info_ref[0]
    hold = info_ref[1]
    own_g = info_ref[2]
    own_r = info_ref[3]
    own_t = info_ref[4]
    scale = LOG2E / math.sqrt(D)
    lane = lax.broadcasted_iota(jnp.int32, (1, D), 1)
    for zz in range(Z):
        for i in range(PROMPT_DEV // D):
            place = (zz * HOLD + hold) * PROMPT_DEV + i * D + lane
            mask = kv_ref[zz, 1024:1040, :].astype(F32)[i : i + 1, :]
            at = zz * PROMPT_DEV + i * D
            for r in range(R):
                seen = (mask > 0.5) & (place < info_ref[5 + r])
                bias_ref[r : r + 1, at : at + D] = jnp.where(seen, 0.0, LOWEST)
    own_keys = own_ref[:, :PLANE, :].reshape(OWN, D)
    own_values = own_ref[:, PLANE:, :].reshape(OWN, D)
    sources = 16
    rows = sources * ROWS
    within = lax.broadcasted_iota(jnp.int32, (sources, ROWS, 1), 1).reshape(rows, 1)
    source = lax.broadcasted_iota(jnp.int32, (sources, ROWS, 1), 0).reshape(rows, 1)
    is_r1 = within >= T * J
    in_r = jnp.where(is_r1, within - T * J, within)
    token = jnp.where(in_r >= J, 1, 0)
    row_r = jnp.where(is_r1, 1, 0)
    own_place = 2 * lax.broadcasted_iota(jnp.int32, (1, OWN), 1) + own_t
    lanes = lax.broadcasted_iota(jnp.int32, (rows, D), 1)
    for tile in range(PLANE // sources):
        row_token = 2 * (z * PLANE + tile * sources + source) + token
        stats = jnp.zeros((rows, D), F32)
        for g in range(G):
            q = q_ref[tile * sources : (tile + 1) * sources, g].astype(F32)
            q = q.reshape(rows, D).astype(BF16)
            keys = kv_ref[:, g * 512 : g * 512 + 256, :].reshape(Z * PROMPT_DEV, D)
            values = kv_ref[:, g * 512 + 256 : g * 512 + 512, :].reshape(Z * PROMPT_DEV, D)
            dims = (((1,), (1,)), ((), ()))
            s = lax.dot_general(q, keys, dims, preferred_element_type=F32) * scale
            s = s + jnp.where(is_r1, bias_ref[1:2, :], bias_ref[0:1, :])
            so = lax.dot_general(q, own_keys, dims, preferred_element_type=F32) * scale
            own_row = jnp.where((row_r == own_r) & (own_g == g), row_token, -1)
            so = jnp.where(own_place <= own_row, so, LOWEST)
            top = jnp.maximum(
                jnp.max(s, axis=1, keepdims=True), jnp.max(so, axis=1, keepdims=True)
            )
            p = jnp.exp2(s - top)
            po = jnp.exp2(so - top)
            total = jnp.sum(p, axis=1, keepdims=True) + jnp.sum(po, axis=1, keepdims=True)
            o = jnp.dot(p.astype(BF16), values, preferred_element_type=F32)
            o = o + jnp.dot(po.astype(BF16), own_values, preferred_element_type=F32)
            o = o / total
            out_ref[tile * sources : (tile + 1) * sources, g * ROWS : (g + 1) * ROWS, :] = (
                o.astype(BF16).reshape(sources, ROWS, D)
            )
            for k, part in enumerate(three_parts(top + jnp.log2(total))):
                stats = jnp.where(lanes == g * 3 + k, part, stats)
        out_ref[tile * sources : (tile + 1) * sources, G * ROWS :, :] = stats.astype(BF16).reshape(
            sources, ROWS, D
        )


def combine_kernel(in_ref, out_ref):
    for h in range(XL * C):
        part = in_ref[:, h].astype(F32)
        for g in range(G):
            stats = part[:, G * ROWS :, :]
            lse = stats[:, :, 3 * g : 3 * g + 1] + stats[:, :, 3 * g + 1 : 3 * g + 2]
            lse = lse + stats[:, :, 3 * g + 2 : 3 * g + 3]
            top = jnp.max(lse, axis=0, keepdims=True)
            w = jnp.exp2(lse - top)
            o = jnp.sum(part[:, g * ROWS : (g + 1) * ROWS, :] * w, axis=0)
            out_ref[h, g] = o / jnp.sum(w, axis=0)


def per_device(
    prompt_keys,
    prompt_values,
    prompt_mask,
    response_queries,
    response_keys,
    response_values,
    resp_lengths,
    prompt_reach,
):
    plane = ("y", "xh", "xl", "c")
    z = lax.axis_index("z")
    y = lax.axis_index("y")
    xh = lax.axis_index("xh")
    hold = y * XH + xh
    kv = jnp.stack([prompt_keys, prompt_values]).transpose(2, 0, 1, 3).reshape(1024, D)
    mask_rows = jnp.pad(prompt_mask.astype(BF16).reshape(2, D), ((0, 14), (0, 0)))
    kv = jnp.concatenate([kv, mask_rows], axis=0)
    kv = lax.all_gather(kv, "z", axis=0, tiled=False)
    heads = XL * C
    q = response_queries.reshape(T, R, heads, G, J, D).transpose(2, 3, 1, 0, 4, 5)
    q = q.reshape(heads, G, LIVE, D)
    own = jnp.stack([response_keys, response_values]).reshape(2, T, R, heads, G, D)
    own = own.transpose(1, 2, 4, 3, 0, 5).reshape(HOLD, heads, 2, D)
    zeros = jnp.zeros((HOLD, heads, 2, D), BF16)
    first = jnp.concatenate(
        [jnp.broadcast_to(q[None, :, 0], (HOLD, heads, LIVE, D)), own, zeros], axis=2
    )
    second = jnp.concatenate(
        [jnp.broadcast_to(q[None, :, 1], (HOLD, heads, LIVE, D)), zeros, zeros], axis=2
    )
    message = jnp.stack([first, second], axis=2).reshape(PLANE, G * ROWS, D)
    rows = lax.all_to_all(message, plane, 0, 0, tiled=True)
    own_rows = jnp.concatenate([rows[:, LIVE], rows[:, LIVE + 1]], axis=0)
    own_rows = jnp.broadcast_to(own_rows[None], (Z, 2 * PLANE, D))
    own_rows = lax.all_to_all(own_rows, "z", 0, 0, tiled=True)
    info = jnp.stack(
        [z, hold, hold % 2, (hold // 2) % 2, hold // 4, prompt_reach[0], prompt_reach[1]]
    ).astype(jnp.int32)
    vmem = pl.BlockSpec(memory_space=pltpu.VMEM)
    partial = pl.pallas_call(
        attend_kernel,
        out_shape=jax.ShapeDtypeStruct((PLANE, (G + 1) * ROWS, D), BF16),
        in_specs=[pl.BlockSpec(memory_space=pltpu.SMEM), vmem, vmem, vmem],
        out_specs=vmem,
        scratch_shapes=[pltpu.VMEM((8, Z * PROMPT_DEV), F32)],
        compiler_params=pltpu.CompilerParams(vmem_limit_bytes=40 << 20),
        name="attend",
    )(info, rows.reshape(PLANE, G, ROWS, D), kv, own_rows)
    partial = lax.all_to_all(partial, plane, 0, 0, tiled=True)
    attended = pl.pallas_call(
        combine_kernel,
        out_shape=jax.ShapeDtypeStruct((heads, G, ROWS, D), F32),
        in_specs=[vmem],
        out_specs=vmem,
        name="combine",
    )(partial.reshape(HOLD, heads, (G + 1) * ROWS, D))
    attended = attended[:, :, :LIVE].reshape(heads, G, R, T, J, D).transpose(3, 2, 0, 1, 4, 5)
    first_row = 2 * ((z * HOLD + hold) * heads + lax.axis_index(("xl", "c")))
    live = (first_row + jnp.arange(T, dtype=jnp.int32))[:, None] < resp_lengths[None, :]
    attended = jnp.where(live[:, :, None, None], attended.reshape(T, R, heads * G * J, D), 0.0)
    return attended.astype(BF16)


def solution(mesh):
    fine = Mesh(mesh.devices.reshape(Z, Y, XH, XL, C), ("z", "y", "xh", "xl", "c"))
    ctx, head = ("z", "y", "xh"), ("xl", "c")
    return jax.shard_map(
        per_device,
        mesh=fine,
        in_specs=(
            P(ctx, head, None),
            P(ctx, head, None),
            P(ctx),
            P(ctx + head, None, None, None),
            P(ctx + head, None, None, None),
            P(ctx + head, None, None, None),
            P(),
            P(),
        ),
        out_specs=P(ctx + head, None, None, None),
        check_vma=False,
    )
```

```python
import functools
import math

import jax
import jax.numpy as jnp
from jax import lax
from jax.experimental import pallas as pl
from jax.experimental.pallas import tpu as pltpu
from jax.sharding import Mesh, PartitionSpec as P

Z, Y, XH, XL, C = 8, 4, 2, 2, 2
HEADS = XL * C
PLANE = Z * HEADS
HOLD = Y * XH
T, R, G, J, D = 2, 2, 2, 5, 128
LIVE = R * T * J
ROWS = 24
OWN = HOLD * PLANE
BLOCK = 256
SOURCES = 16
TILE = SOURCES * ROWS
TILES = PLANE // SOURCES
LOWEST = -1e30
LOG2E = math.log2(math.e)
F32 = jnp.float32
BF16 = jnp.bfloat16
FIRST = ((0, 0), (3, 0), (1, 0), (2, 0), (0, 1))
SECOND = ((3, 1), (1, 1), (2, 1))
CONTRACT_LAST = (((1,), (1,)), ((), ()))


def three_parts(x):
    hi = x.astype(BF16).astype(F32)
    mid = (x - hi).astype(BF16).astype(F32)
    lo = (x - hi - mid).astype(BF16).astype(F32)
    return hi, mid, lo


def fill_bias(info_ref, kv_refs, offsets, bias_ref):
    z, y, xh = info_ref[0], info_ref[1], info_ref[2]
    lane = lax.broadcasted_iota(jnp.int32, (1, D), 1)
    for b, (kv_ref, (dy, dx)) in enumerate(zip(kv_refs, offsets)):
        ctx = z * HOLD + lax.rem(y + dy, Y) * XH + lax.rem(xh + dx, XH)
        mask = kv_ref[1024:1040, :].astype(F32)
        for i in range(BLOCK // D):
            place = ctx * BLOCK + i * D + lane
            at = b * BLOCK + i * D
            for r in range(R):
                seen = (mask[i : i + 1, :] > 0.5) & (place < info_ref[3 + r])
                bias_ref[r : r + 1, at : at + D] = jnp.where(seen, 0.0, LOWEST)


def row_parts():
    within = lax.broadcasted_iota(jnp.int32, (SOURCES, ROWS, 1), 1).reshape(TILE, 1)
    source = lax.broadcasted_iota(jnp.int32, (SOURCES, ROWS, 1), 0).reshape(TILE, 1)
    return within, source


def tile_queries(q_ref, tile, g):
    q = q_ref[tile * SOURCES : (tile + 1) * SOURCES, g].astype(F32)
    return q.reshape(TILE, D).astype(BF16)


def block_scores(q, kv_refs, g, bias_ref, is_r1):
    scale = LOG2E / math.sqrt(D)
    scores = []
    for b, kv_ref in enumerate(kv_refs):
        keys = kv_ref[g * 2 * BLOCK : g * 2 * BLOCK + BLOCK, :]
        s = lax.dot_general(q, keys, CONTRACT_LAST, preferred_element_type=F32) * scale
        at = slice(b * BLOCK, (b + 1) * BLOCK)
        scores.append(s + jnp.where(is_r1, bias_ref[1:2, at], bias_ref[0:1, at]))
    return scores


def block_values(kv_refs, g):
    return [kv_ref[g * 2 * BLOCK + BLOCK : (g + 1) * 2 * BLOCK, :] for kv_ref in kv_refs]


def weigh(scores, values, top):
    total, summed = 0.0, 0.0
    for s, v in zip(scores, values):
        p = jnp.exp2(s - top)
        total = total + jnp.sum(p, axis=1, keepdims=True)
        summed = summed + jnp.dot(p.astype(BF16), v, preferred_element_type=F32)
    return total, summed


def top_of(scores):
    wide = functools.reduce(jnp.maximum, scores)
    return jnp.max(wide, axis=1, keepdims=True)


def first_kernel(info_ref, q_ref, *refs):
    kv_refs, (acc_ref, stat_ref, bias_ref) = refs[: len(FIRST)], refs[len(FIRST) :]
    fill_bias(info_ref, kv_refs, FIRST, bias_ref)
    within, _ = row_parts()
    lanes = lax.broadcasted_iota(jnp.int32, (TILE, D), 1)
    for tile in range(TILES):
        for g in range(G):
            q = tile_queries(q_ref, tile, g)
            scores = block_scores(q, kv_refs, g, bias_ref, within >= T * J)
            top = top_of(scores)
            total, summed = weigh(scores, block_values(kv_refs, g), top)
            acc_ref[tile, g] = summed
            stat_ref[tile, g] = jnp.where(lanes == 0, top, total)


def second_kernel(info_ref, q_ref, *refs):
    kv_refs, (own_ref, acc_ref, stat_ref, out_ref, bias_ref) = refs[: len(SECOND)], refs[len(SECOND) :]
    z, y, xh = info_ref[0], info_ref[1], info_ref[2]
    fill_bias(info_ref, kv_refs, SECOND, bias_ref)
    own_keys = own_ref[:, :PLANE, :].reshape(OWN, D)
    own_values = own_ref[:, PLANE:, :].reshape(OWN, D)
    within, source = row_parts()
    is_r1 = within >= T * J
    in_r = jnp.where(is_r1, within - T * J, within)
    row_r = jnp.where(is_r1, 1, 0)
    row_t = jnp.where(in_r >= J, 1, 0)
    k = lax.broadcasted_iota(jnp.int32, (1, OWN), 1)
    own_device = ((k >> 2) & (Z - 1)) * HOLD * HEADS + (k >> 5) * HEADS + (k & (HEADS - 1))
    own_place = 2 * own_device + (z >> 2)
    lanes = lax.broadcasted_iota(jnp.int32, (TILE, D), 1)
    for tile in range(TILES):
        from_source = tile * SOURCES + source
        row_device = (from_source >> 2) * HOLD * HEADS + (y * XH + xh) * HEADS + (from_source & (HEADS - 1))
        row_place = 2 * row_device + row_t
        stats = jnp.zeros((TILE, D), F32)
        outs = []
        for g in range(G):
            q = tile_queries(q_ref, tile, g)
            scores = block_scores(q, kv_refs, g, bias_ref, is_r1)
            so = lax.dot_general(q, own_keys, CONTRACT_LAST, preferred_element_type=F32)
            so = so * (LOG2E / math.sqrt(D))
            own_row = jnp.where((row_r == ((z >> 1) & 1)) & ((z & 1) == g), row_place, -1)
            scores.append(jnp.where(own_place <= own_row, so, LOWEST))
            before = stat_ref[tile, g]
            top_before, total_before = before[:, 0:1], before[:, 1:2]
            top = jnp.maximum(top_of(scores), top_before)
            total, summed = weigh(scores, block_values(kv_refs, g) + [own_values], top)
            shrink = jnp.exp2(top_before - top)
            total = total + total_before * shrink
            summed = (summed + acc_ref[tile, g] * shrink) / total
            outs.append(summed.reshape(SOURCES, ROWS, D))
            for i, part in enumerate(three_parts(top + jnp.log2(total))):
                stats = jnp.where(lanes == (g * 3 + i) * LIVE + within, part, stats)
        stats = jnp.where(within < LIVE, stats, 0.0).reshape(SOURCES, ROWS, D)
        stats = jnp.sum(stats, axis=1, keepdims=True)
        spare = lax.broadcasted_iota(jnp.int32, (SOURCES, ROWS, D), 1) == LIVE
        at = slice(tile * SOURCES, (tile + 1) * SOURCES)
        out_ref[at, 0] = jnp.where(spare, stats, outs[0]).astype(BF16)
        out_ref[at, 1] = outs[1].astype(BF16)


def combine_kernel(in_ref, out_ref):
    lane = lax.broadcasted_iota(jnp.int32, (1, ROWS, D), 2)
    row = lax.broadcasted_iota(jnp.int32, (1, ROWS, D), 1)
    for h in range(HEADS):
        parts = [in_ref[:, h, g].astype(F32) for g in range(G)]
        stats = parts[0][:, LIVE : LIVE + 1, :]
        for g in range(G):
            mine = False
            for i in range(3):
                mine = mine | (lane == (g * 3 + i) * LIVE + row)
            mine = mine & (row < LIVE)
            lse = jnp.sum(jnp.where(mine, stats, 0.0), axis=2, keepdims=True)
            top = jnp.max(lse, axis=0, keepdims=True)
            w = jnp.exp2(lse - top)
            out_ref[h, g] = jnp.sum(parts[g] * w, axis=0) / jnp.sum(w, axis=0)


def permute(x, axis, size, shift):
    return lax.ppermute(x, axis, [(i, (i + shift) % size) for i in range(size)])


def per_device(
    prompt_keys,
    prompt_values,
    prompt_mask,
    response_queries,
    response_keys,
    response_values,
    resp_lengths,
    prompt_reach,
):
    plane = ("z", "xl", "c")
    z = lax.axis_index("z")
    y = lax.axis_index("y")
    xh = lax.axis_index("xh")
    q = response_queries.reshape(T, R, HEADS, G, J, D).transpose(2, 3, 1, 0, 4, 5)
    q = q.reshape(HEADS, G, LIVE, D)
    own = jnp.stack([response_keys, response_values]).reshape(2, T, R, HEADS, G, D)
    own = own.transpose(1, 2, 4, 3, 0, 5).reshape(Z, HEADS, 2, D)
    zeros = jnp.zeros((Z, HEADS, 2, D), BF16)
    first = jnp.concatenate(
        [jnp.broadcast_to(q[None, :, 0], (Z, HEADS, LIVE, D)), own, zeros], axis=2
    )
    second = jnp.concatenate(
        [jnp.broadcast_to(q[None, :, 1], (Z, HEADS, LIVE, D)), zeros, zeros], axis=2
    )
    message = jnp.stack([first, second], axis=2).reshape(PLANE, G * ROWS, D)
    rows = lax.all_to_all(message, plane, 0, 0, tiled=True)
    kv = jnp.stack([prompt_keys, prompt_values]).transpose(2, 0, 1, 3).reshape(4 * BLOCK, D)
    mask_rows = jnp.pad(prompt_mask.astype(BF16).reshape(2, D), ((0, 14), (0, 0)))
    kv = jnp.concatenate([kv, mask_rows], axis=0)
    before = permute(kv, "y", Y, 1)
    after = permute(kv, "y", Y, 3)
    far = permute(kv, "y", Y, 2)
    across = permute(kv, "xh", XH, 1)
    rows, before, after, far, across = lax.optimization_barrier((rows, before, after, far, across))
    across_before = permute(across, "y", Y, 1)
    across_after = permute(across, "y", Y, 3)
    across_far = permute(far, "xh", XH, 1)
    own_rows = jnp.concatenate([rows[:, LIVE], rows[:, LIVE + 1]], axis=0)
    own_rows = jnp.broadcast_to(own_rows[None], (HOLD, 2 * PLANE, D))
    own_rows = lax.all_to_all(own_rows, ("y", "xh"), 0, 0, tiled=True)
    info = jnp.stack([z, y, xh, prompt_reach[0], prompt_reach[1]]).astype(jnp.int32)
    smem = pl.BlockSpec(memory_space=pltpu.SMEM)
    vmem = pl.BlockSpec(memory_space=pltpu.VMEM)
    rows = rows.reshape(PLANE, G, ROWS, D)
    pair_flops = 4 * PLANE * G * ROWS * BLOCK * D
    acc, stat = pl.pallas_call(
        first_kernel,
        out_shape=[jax.ShapeDtypeStruct((TILES, G, TILE, D), F32)] * 2,
        in_specs=[smem] + [vmem] * (1 + len(FIRST)),
        out_specs=[vmem] * 2,
        scratch_shapes=[pltpu.VMEM((8, len(FIRST) * BLOCK), F32)],
        compiler_params=pltpu.CompilerParams(vmem_limit_bytes=40 << 20),
        cost_estimate=pl.CostEstimate(
            flops=len(FIRST) * pair_flops, bytes_accessed=3 << 20, transcendentals=len(FIRST) * pair_flops // 512
        ),
        name="attend_first",
    )(info, rows, kv, before, after, far, across)
    partial = pl.pallas_call(
        second_kernel,
        out_shape=jax.ShapeDtypeStruct((PLANE, G, ROWS, D), BF16),
        in_specs=[smem] + [vmem] * (4 + len(SECOND)),
        out_specs=vmem,
        scratch_shapes=[pltpu.VMEM((8, len(SECOND) * BLOCK), F32)],
        compiler_params=pltpu.CompilerParams(vmem_limit_bytes=40 << 20),
        cost_estimate=pl.CostEstimate(
            flops=4 * pair_flops, bytes_accessed=3 << 20, transcendentals=4 * pair_flops // 512
        ),
        name="attend_second",
    )(info, rows, across_before, across_after, across_far, own_rows, acc, stat)
    partial = lax.all_to_all(partial.reshape(PLANE, G * ROWS, D), plane, 0, 0, tiled=True)
    attended = pl.pallas_call(
        combine_kernel,
        out_shape=jax.ShapeDtypeStruct((HEADS, G, ROWS, D), F32),
        in_specs=[vmem],
        out_specs=vmem,
        name="combine",
    )(partial.reshape(Z, HEADS, G, ROWS, D))
    attended = attended[:, :, :LIVE].reshape(HEADS, G, R, T, J, D).transpose(3, 2, 0, 1, 4, 5)
    first_row = T * (((z * Y + y) * XH + xh) * HEADS + lax.axis_index(("xl", "c")))
    live = (first_row + jnp.arange(T, dtype=jnp.int32))[:, None] < resp_lengths[None, :]
    attended = jnp.where(live[:, :, None, None], attended.reshape(T, R, HEADS * G * J, D), 0.0)
    return attended.astype(BF16)


def solution(mesh):
    fine = Mesh(mesh.devices.reshape(Z, Y, XH, XL, C), ("z", "y", "xh", "xl", "c"))
    ctx, head = ("z", "y", "xh"), ("xl", "c")
    return jax.shard_map(
        per_device,
        mesh=fine,
        in_specs=(
            P(ctx, head, None),
            P(ctx, head, None),
            P(ctx),
            P(ctx + head, None, None, None),
            P(ctx + head, None, None, None),
            P(ctx + head, None, None, None),
            P(),
            P(),
        ),
        out_specs=P(ctx + head, None, None, None),
        check_vma=False,
    )
```

```python
import functools
import math

import jax
import jax.numpy as jnp
import numpy as np
from jax import lax
from jax.experimental import pallas as pl
from jax.experimental.pallas import tpu as pltpu
from jax.sharding import Mesh, PartitionSpec as P

Z, Y, XH, XL, C = 8, 4, 2, 2, 2
HEADS = XL * C
PLANE = Z * HEADS
HOLD = Y * XH
T, R, G, J, D = 2, 2, 2, 5, 128
LIVE = R * T * J
ROWS = 24
BLOCK = 256
QUERIES = T * R * HEADS * G * J
MESSAGE = HEADS * G * ROWS
MASK = 4 * BLOCK
OWN = MASK + 16
OWN_ROWS = 16
PACK = OWN + 2 * G * OWN_ROWS
SOURCES = 16
TILE = SOURCES * ROWS
TILES = PLANE // SOURCES
LOWEST = -1e30
LOG2E = math.log2(math.e)
F32 = jnp.float32
BF16 = jnp.bfloat16
FIRST = ((0, 0), (3, 0), (1, 0), (2, 0), (0, 1))
SECOND = ((3, 1), (1, 1), (2, 1))
CONTRACT_LAST = (((1,), (1,)), ((), ()))


def three_parts(x):
    hi = x.astype(BF16).astype(F32)
    mid = (x - hi).astype(BF16).astype(F32)
    lo = (x - hi - mid).astype(BF16).astype(F32)
    return hi, mid, lo


def ctx_of(offset):
    dy, dx = offset
    y = lax.rem(lax.axis_index("y") + dy, Y)
    xh = lax.rem(lax.axis_index("xh") + dx, XH)
    return (lax.axis_index("z") * Y + y) * XH + xh


def fill_bias(reach_ref, kv_refs, offsets, bias_ref):
    lane = lax.broadcasted_iota(jnp.int32, (1, D), 1)
    for b, (kv_ref, offset) in enumerate(zip(kv_refs, offsets)):
        ctx = ctx_of(offset)
        mask = kv_ref[MASK:OWN, :].astype(F32)
        for i in range(BLOCK // D):
            place = ctx * BLOCK + i * D + lane
            at = b * BLOCK + i * D
            for r in range(R):
                seen = (mask[i : i + 1, :] > 0.5) & (place < reach_ref[r])
                bias_ref[r : r + 1, at : at + D] = jnp.where(seen, 0.0, LOWEST)


def row_parts():
    within = lax.broadcasted_iota(jnp.int32, (SOURCES, ROWS, 1), 1).reshape(TILE, 1)
    source = lax.broadcasted_iota(jnp.int32, (SOURCES, ROWS, 1), 0).reshape(TILE, 1)
    return within, source


def tile_queries(q_ref, tile, g):
    q = q_ref[tile * SOURCES : (tile + 1) * SOURCES, g].astype(F32)
    return q.reshape(TILE, D).astype(BF16)


def block_scores(q, kv_refs, g, bias_ref, is_r1):
    scale = LOG2E / math.sqrt(D)
    scores = []
    for b, kv_ref in enumerate(kv_refs):
        keys = kv_ref[g * 2 * BLOCK : g * 2 * BLOCK + BLOCK, :]
        s = lax.dot_general(q, keys, CONTRACT_LAST, preferred_element_type=F32) * scale
        at = slice(b * BLOCK, (b + 1) * BLOCK)
        scores.append(s + jnp.where(is_r1, bias_ref[1:2, at], bias_ref[0:1, at]))
    return scores


def block_values(kv_refs, g):
    return [kv_ref[g * 2 * BLOCK + BLOCK : (g + 1) * 2 * BLOCK, :] for kv_ref in kv_refs]


def weigh(scores, values, top):
    total, summed = 0.0, 0.0
    for s, v in zip(scores, values):
        p = jnp.exp2(s - top)
        total = total + jnp.sum(p, axis=1, keepdims=True)
        summed = summed + jnp.dot(p.astype(BF16), v, preferred_element_type=F32)
    return total, summed


def top_of(scores):
    wide = functools.reduce(jnp.maximum, scores)
    return jnp.max(wide, axis=1, keepdims=True)


def first_kernel(reach_ref, q_ref, *refs):
    kv_refs, (acc_ref, stat_ref, bias_ref) = refs[: len(FIRST)], refs[len(FIRST) :]
    fill_bias(reach_ref, kv_refs, FIRST, bias_ref)
    within, _ = row_parts()
    lanes = lax.broadcasted_iota(jnp.int32, (TILE, D), 1)
    for tile in range(TILES):
        for g in range(G):
            q = tile_queries(q_ref, tile, g)
            scores = block_scores(q, kv_refs, g, bias_ref, within >= T * J)
            top = top_of(scores)
            total, summed = weigh(scores, block_values(kv_refs, g), top)
            acc_ref[tile, g] = summed
            stat_ref[tile, g] = jnp.where(lanes == 0, top, total)


def second_kernel(reach_ref, q_ref, *refs):
    all_refs, (acc_ref, stat_ref, out_ref, bias_ref) = refs[:HOLD], refs[HOLD:]
    kv_refs = all_refs[len(FIRST) :]
    fill_bias(reach_ref, kv_refs, SECOND, bias_ref)
    within, source = row_parts()
    is_r1 = within >= T * J
    in_r = jnp.where(is_r1, within - T * J, within)
    row_r = jnp.where(is_r1, 1, 0)
    row_t = jnp.where(in_r >= J, 1, 0)
    k = lax.broadcasted_iota(jnp.int32, (1, HOLD * OWN_ROWS), 1)
    own_ctx = jnp.zeros((1, HOLD * OWN_ROWS), jnp.int32)
    for b, offset in enumerate(FIRST + SECOND):
        own_ctx = jnp.where((k >> 4) == b, ctx_of(offset), own_ctx)
    own_place = T * (own_ctx * HEADS + ((k >> 2) & 3)) + (k & 1)
    own_r = (k >> 1) & 1
    lanes = lax.broadcasted_iota(jnp.int32, (TILE, D), 1)
    here = lax.axis_index("y") * XH + lax.axis_index("xh")
    for tile in range(TILES):
        from_source = tile * SOURCES + source
        row_device = ((from_source >> 2) * HOLD + here) * HEADS + (from_source & 3)
        row_place = T * row_device + row_t
        seen = (own_r == row_r) & (own_place <= row_place)
        stats = jnp.zeros((TILE, D), F32)
        outs = []
        for g in range(G):
            q = tile_queries(q_ref, tile, g)
            scores = block_scores(q, kv_refs, g, bias_ref, is_r1)
            at = OWN + g * OWN_ROWS
            own_keys = jnp.concatenate([ref[at : at + OWN_ROWS, :] for ref in all_refs], axis=0)
            at = at + G * OWN_ROWS
            own_values = jnp.concatenate([ref[at : at + OWN_ROWS, :] for ref in all_refs], axis=0)
            so = lax.dot_general(q, own_keys, CONTRACT_LAST, preferred_element_type=F32)
            so = jnp.where(seen, so * (LOG2E / math.sqrt(D)), LOWEST)
            before = stat_ref[tile, g]
            top_before, total_before = before[:, 0:1], before[:, 1:2]
            top = jnp.maximum(top_of(scores), jnp.max(so, axis=1, keepdims=True))
            top = jnp.maximum(top, top_before)
            values = block_values(kv_refs, g) + [own_values]
            total, summed = weigh(scores + [so], values, top)
            shrink = jnp.exp2(top_before - top)
            total = total + total_before * shrink
            summed = (summed + acc_ref[tile, g] * shrink) * (1.0 / total)
            outs.append(summed.reshape(SOURCES, ROWS, D))
            for i, part in enumerate(three_parts(top + jnp.log2(total))):
                stats = jnp.where(lanes == (g * 3 + i) * LIVE + within, part, stats)
        stats = jnp.where(within < LIVE, stats, 0.0).reshape(SOURCES, ROWS, D)
        stats = jnp.sum(stats, axis=1, keepdims=True)
        spare = lax.broadcasted_iota(jnp.int32, (SOURCES, ROWS, D), 1) == LIVE
        at = slice(tile * SOURCES, (tile + 1) * SOURCES)
        out_ref[at, 0] = jnp.where(spare, stats, outs[0]).astype(BF16)
        out_ref[at, 1] = outs[1].astype(BF16)


def combine_kernel(lengths_ref, order_ref, in_ref, out_ref, rows_ref):
    lane = lax.broadcasted_iota(jnp.int32, (1, ROWS, D), 2)
    row = lax.broadcasted_iota(jnp.int32, (1, ROWS, D), 1)
    for h in range(HEADS):
        parts = [in_ref[:, h, g].astype(F32) for g in range(G)]
        stats = parts[0][:, LIVE : LIVE + 1, :]
        for g in range(G):
            mine = False
            for i in range(3):
                mine = mine | (lane == (g * 3 + i) * LIVE + row)
            mine = mine & (row < LIVE)
            lse = jnp.sum(jnp.where(mine, stats, 0.0), axis=2, keepdims=True)
            top = jnp.max(lse, axis=0, keepdims=True)
            w = jnp.exp2(lse - top)
            o = jnp.sum(parts[g] * w, axis=0) / jnp.sum(w, axis=0)
            at = (h * G + g) * ROWS
            rows_ref[at : at + ROWS, :] = jnp.where(row[0] < LIVE, o, 0.0)
    rows = jnp.dot(order_ref[...], rows_ref[...].astype(BF16), preferred_element_type=F32)
    heads = HEADS * G * J
    first = T * (ctx_of((0, 0)) * HEADS + lax.axis_index("xl") * C + lax.axis_index("c"))
    for t in range(T):
        for r in range(R):
            at = (t * R + r) * heads
            live = first + t < lengths_ref[r]
            out_ref[t, r] = jnp.where(live, rows[at : at + heads, :], 0.0).astype(BF16)


def message_order():
    order = np.zeros((MESSAGE, QUERIES), np.float32)
    for h in range(HEADS):
        for g in range(G):
            for r in range(R):
                for t in range(T):
                    for j in range(J):
                        to = (h * G + g) * ROWS + (r * T + t) * J + j
                        order[to, (t * R + r) * HEADS * G * J + (h * G + g) * J + j] = 1
    return order


def own_order():
    kv_heads = HEADS * G
    order = np.zeros((2 * T * R * kv_heads, 2 * T * R * kv_heads), np.float32)
    for h in range(HEADS):
        for kv in range(2):
            for g in range(G):
                for r in range(R):
                    for t in range(T):
                        to = ((h * 2 + kv) * G + g) * R * T + r * T + t
                        order[to, (kv * T * R + t * R + r) * kv_heads + h * G + g] = 1
    return order


def message_kernel(order_ref, own_order_ref, q_ref, k_ref, v_ref, message_ref, *refs):
    own_refs, own_rows = refs[:HEADS], refs[HEADS]
    q = q_ref[...].astype(F32).reshape(QUERIES, D).astype(BF16)
    rows = jnp.dot(order_ref[...], q, preferred_element_type=F32).astype(BF16)
    for z in range(Z):
        message_ref[z] = rows
    own = [ref[...].astype(F32).reshape(T * R * HEADS * G, D) for ref in (k_ref, v_ref)]
    own = jnp.concatenate(own, axis=0).astype(BF16)
    own = jnp.dot(own_order_ref[...], own, preferred_element_type=F32)
    own_rows[...] = own.reshape(HEADS, own.shape[0] // HEADS, D)
    head = lax.axis_index("xl") * C + lax.axis_index("c")
    for step, own_ref in enumerate(own_refs):
        own_ref[...] = own_rows[lax.rem(head + step, HEADS)].astype(BF16)


def pack_kernel(mask_ref, k_ref, v_ref, *refs):
    own_refs, (pack_ref, wide, by_head, sorted_rows) = refs[:HEADS], refs[HEADS:]
    for kv, ref in enumerate((k_ref, v_ref)):
        wide[kv] = ref[...].astype(F32)
        for g in range(G):
            at = (g * 2 + kv) * BLOCK
            pack_ref[at : at + BLOCK, :] = wide[kv, pl.ds(g, BLOCK, stride=G), :].astype(BF16)
    head = lax.axis_index("xl") * C + lax.axis_index("c")
    for step, own_ref in enumerate(own_refs):
        by_head[lax.rem(head + HEADS - step, HEADS)] = own_ref[...].astype(F32)
    part = T * R
    for h in range(HEADS):
        for kind in range(2 * G):
            at = kind * OWN_ROWS + h * part
            sorted_rows[at : at + part, :] = by_head[h, kind * part : (kind + 1) * part, :]
    pack_ref[OWN:PACK, :] = sorted_rows[...].astype(BF16)
    by_head[0] = jnp.zeros((16, D), F32)
    by_head[0, 0 : BLOCK // D, :] = mask_ref[...].astype(F32)
    pack_ref[MASK:OWN, :] = by_head[0].astype(BF16)


def permute(x, axis, size, shift):
    return lax.ppermute(x, axis, [(i, (i + shift) % size) for i in range(size)])


def per_device(
    prompt_keys,
    prompt_values,
    prompt_mask,
    response_queries,
    response_keys,
    response_values,
    resp_lengths,
    prompt_reach,
):
    plane = ("z", "xl", "c")
    head = ("xl", "c")
    smem = pl.BlockSpec(memory_space=pltpu.SMEM)
    vmem = pl.BlockSpec(memory_space=pltpu.VMEM)
    order = message_order()
    own_part = 2 * G * T * R
    message, *own = pl.pallas_call(
        message_kernel,
        out_shape=[jax.ShapeDtypeStruct((Z, MESSAGE, D), BF16)]
        + [jax.ShapeDtypeStruct((own_part, D), BF16)] * HEADS,
        in_specs=[vmem] * 5,
        out_specs=[vmem] * (1 + HEADS),
        scratch_shapes=[pltpu.VMEM((HEADS, own_part, D), F32)],
        name="message",
    )(
        jnp.asarray(order, BF16),
        jnp.asarray(own_order(), BF16),
        response_queries,
        response_keys,
        response_values,
    )
    own = [own[0]] + [permute(own[step], head, HEADS, step) for step in range(1, HEADS)]
    rows = lax.all_to_all(message.reshape(PLANE, G * ROWS, D), plane, 0, 0, tiled=True)
    kv = pl.pallas_call(
        pack_kernel,
        out_shape=jax.ShapeDtypeStruct((PACK, D), BF16),
        in_specs=[vmem] * (3 + HEADS),
        out_specs=vmem,
        scratch_shapes=[
            pltpu.VMEM((2, G * BLOCK, D), F32),
            pltpu.VMEM((HEADS, own_part, D), F32),
            pltpu.VMEM((HEADS * own_part, D), F32),
        ],
        name="pack",
    )(
        prompt_mask.reshape(BLOCK // D, D),
        prompt_keys.reshape(BLOCK * G, D),
        prompt_values.reshape(BLOCK * G, D),
        *own,
    )
    across = permute(kv, "xh", XH, 1)
    far = permute(kv, "y", Y, 2)
    before = permute(kv, "y", Y, 1)
    after = permute(kv, "y", Y, 3)
    across_before = permute(across, "y", Y, 1)
    across_after = permute(across, "y", Y, 3)
    across_far = permute(far, "xh", XH, 1)
    rows = rows.reshape(PLANE, G, ROWS, D)
    first_blocks = (kv, before, after, far, across)
    second_blocks = (across_before, across_after, across_far)
    pair_flops = 4 * PLANE * G * ROWS * BLOCK * D
    acc, stat = pl.pallas_call(
        first_kernel,
        out_shape=[jax.ShapeDtypeStruct((TILES, G, TILE, D), F32)] * 2,
        in_specs=[smem] + [vmem] * (1 + len(FIRST)),
        out_specs=[vmem] * 2,
        scratch_shapes=[pltpu.VMEM((8, len(FIRST) * BLOCK), F32)],
        compiler_params=pltpu.CompilerParams(vmem_limit_bytes=24 << 20),
        cost_estimate=pl.CostEstimate(
            flops=len(FIRST) * pair_flops,
            bytes_accessed=3 << 20,
            transcendentals=len(FIRST) * pair_flops // 512,
        ),
        name="attend_first",
    )(prompt_reach, rows, *first_blocks)
    partial = pl.pallas_call(
        second_kernel,
        out_shape=jax.ShapeDtypeStruct((PLANE, G, ROWS, D), BF16),
        in_specs=[smem] + [vmem] * (3 + HOLD),
        out_specs=vmem,
        scratch_shapes=[pltpu.VMEM((8, len(SECOND) * BLOCK), F32)],
        compiler_params=pltpu.CompilerParams(vmem_limit_bytes=24 << 20),
        cost_estimate=pl.CostEstimate(
            flops=4 * pair_flops, bytes_accessed=3 << 20, transcendentals=4 * pair_flops // 512
        ),
        name="attend_second",
    )(prompt_reach, rows, *first_blocks, *second_blocks, acc, stat)
    partial = lax.all_to_all(partial.reshape(PLANE, G * ROWS, D), plane, 0, 0, tiled=True)
    return pl.pallas_call(
        combine_kernel,
        out_shape=jax.ShapeDtypeStruct((T, R, HEADS * G * J, D), BF16),
        in_specs=[smem, vmem, vmem],
        out_specs=vmem,
        scratch_shapes=[pltpu.VMEM((MESSAGE, D), F32)],
        name="combine",
    )(resp_lengths, jnp.asarray(order.T, BF16), partial.reshape(Z, HEADS, G, ROWS, D))


def solution(mesh):
    fine = Mesh(mesh.devices.reshape(Z, Y, XH, XL, C), ("z", "y", "xh", "xl", "c"))
    ctx, head = ("z", "y", "xh"), ("xl", "c")
    return jax.shard_map(
        per_device,
        mesh=fine,
        in_specs=(
            P(ctx, head, None),
            P(ctx, head, None),
            P(ctx),
            P(ctx + head, None, None, None),
            P(ctx + head, None, None, None),
            P(ctx + head, None, None, None),
            P(),
            P(),
        ),
        out_specs=P(ctx + head, None, None, None),
        check_vma=False,
    )
```

```python
import functools
import math

import jax
import jax.numpy as jnp
import numpy as np
from jax import lax
from jax.experimental import pallas as pl
from jax.experimental.pallas import tpu as pltpu
from jax.sharding import Mesh, PartitionSpec as P

Z, Y, XH, XL, C = 8, 4, 2, 2, 2
HEADS = XL * C
PLANE = Z * HEADS
HOLD = Y * XH
T, R, G, J, D = 2, 2, 2, 5, 128
LIVE = R * T * J
ROWS = 24
BLOCK = 256
QUERIES = T * R * HEADS * G * J
MESSAGE = HEADS * G * ROWS
MASK = 4 * BLOCK
PACK = MASK + 16
OWN_PART = 2 * G * R * T
NEAR = HOLD * HEADS
BLOCKS = ((0, 0), (3, 0), (1, 0), (2, 0), (0, 1), (3, 1), (1, 1), (2, 1))
SOURCES = 16
TILE = SOURCES * ROWS
TILES = PLANE // SOURCES
LOWEST = -1e30
LOG2E = math.log2(math.e)
F32 = jnp.float32
BF16 = jnp.bfloat16
CONTRACT_LAST = (((1,), (1,)), ((), ()))


def three_parts(x):
    hi = x.astype(BF16).astype(F32)
    mid = (x - hi).astype(BF16).astype(F32)
    lo = (x - hi - mid).astype(BF16).astype(F32)
    return hi, mid, lo


def ctx_of(offset):
    dy, dx = offset
    y = lax.rem(lax.axis_index("y") + dy, Y)
    xh = lax.rem(lax.axis_index("xh") + dx, XH)
    return (lax.axis_index("z") * Y + y) * XH + xh


def row_parts():
    lane = lax.broadcasted_iota(jnp.int32, (1, TILE), 1)
    source = (lane * 2731) >> 16
    return source, lane - source * ROWS


def fill_bias(reach_ref, kv_refs, bias_ref):
    lane = lax.broadcasted_iota(jnp.int32, (1, D), 1)
    sub = lax.broadcasted_iota(jnp.int32, (8, D), 0)
    _, within = row_parts()
    row_r = jnp.where(within >= T * J, 1, 0)
    pick = (lax.broadcasted_iota(jnp.int32, (8, TILE), 0) == row_r).astype(F32).astype(BF16)
    for b, (kv_ref, offset) in enumerate(zip(kv_refs, BLOCKS)):
        ctx = ctx_of(offset)
        mask = kv_ref[MASK:PACK, :].astype(F32)
        for i in range(BLOCK // D):
            place = ctx * BLOCK + i * D + lane
            reach = jnp.where(sub == 0, reach_ref[0], reach_ref[1])
            seen = (mask[i : i + 1, :] > 0.5) & (place < reach)
            hide = jnp.where(seen, 0.0, LOWEST).astype(BF16)
            bias_ref[b, i * D : (i + 1) * D, :] = lax.dot_general(
                hide, pick, (((0,), (0,)), ((), ())), preferred_element_type=F32
            )


def tile_queries(q_ref, tile, g):
    q = q_ref[tile * SOURCES : (tile + 1) * SOURCES, g].astype(F32)
    return q.reshape(TILE, D).astype(BF16)


def block_scores(q, kv_refs, g, bias_ref):
    scores = []
    for b, kv_ref in enumerate(kv_refs):
        keys = kv_ref[g * 2 * BLOCK : g * 2 * BLOCK + BLOCK, :]
        s = lax.dot_general(keys, q, CONTRACT_LAST, preferred_element_type=F32)
        scores.append(s + bias_ref[b])
    return scores


def block_values(kv_refs, g):
    return [kv_ref[g * 2 * BLOCK + BLOCK : (g + 1) * 2 * BLOCK, :] for kv_ref in kv_refs]


def weigh(scores, values, top):
    scale = LOG2E / math.sqrt(D)
    total, summed = 0.0, 0.0
    top = top * scale
    for s, v in zip(scores, values):
        p = jnp.exp2(s * scale - top)
        total = total + jnp.sum(p, axis=0, keepdims=True)
        summed = summed + lax.dot_general(
            v, p.astype(BF16), (((0,), (0,)), ((), ())), preferred_element_type=F32
        )
    return total, summed


def top_of(scores):
    wide = functools.reduce(jnp.maximum, scores)
    return jnp.max(wide, axis=0, keepdims=True)


def finish(outs, lse, tile, out_ref):
    source, within = row_parts()
    mine = lax.broadcasted_iota(jnp.int32, (SOURCES, TILE), 0) == source
    row = lax.broadcasted_iota(jnp.int32, (SOURCES, ROWS, D), 1).reshape(TILE, D)
    lane = lax.broadcasted_iota(jnp.int32, (TILE, D), 1)
    spread = ((row == lane) & (row < LIVE)).astype(F32).astype(BF16)
    stats = 0.0
    for g in range(G):
        for i, part in enumerate(three_parts(lse[g])):
            rows = jnp.where(mine, part, 0.0).astype(BF16)
            rows = jnp.dot(rows, spread, preferred_element_type=F32)
            at = (g * 3 + i) * LIVE
            stats = stats + (pltpu.roll(rows, at, 1) if at else rows)
    at = slice(tile * SOURCES, (tile + 1) * SOURCES)
    spare = lax.broadcasted_iota(jnp.int32, (SOURCES, ROWS, D), 1) == LIVE
    out_ref[at, 0] = jnp.where(spare, stats[:, None, :], outs[0]).astype(BF16)
    out_ref[at, 1] = outs[1].astype(BF16)


def own_seen(tile):
    source, within = row_parts()
    is_r1 = within >= T * J
    in_r = jnp.where(is_r1, within - T * J, within)
    row_r = jnp.where(is_r1, 1, 0)
    row_t = jnp.where(in_r >= J, 1, 0)
    k = lax.broadcasted_iota(jnp.int32, (R * T * NEAR, 1), 0)
    own_place = T * (lax.axis_index("z") * NEAR + (k & (NEAR - 1))) + ((k >> 5) & 1)
    own_r = k >> 6
    here = lax.axis_index("y") * XH + lax.axis_index("xh")
    from_source = tile * SOURCES + source
    row_device = ((from_source >> 2) * HOLD + here) * HEADS + (from_source & 3)
    row_place = T * row_device + row_t
    return (own_r == row_r) & (own_place <= row_place)


def own_part(own_rows, kind):
    at = kind * R * T
    parts = [own_rows[pl.ds(at + e, NEAR, stride=OWN_PART), :] for e in range(R * T)]
    return jnp.concatenate(parts, axis=0).astype(BF16)


def attend_kernel(reach_ref, q_ref, own_ref, *refs):
    kv_refs, (out_ref, bias_ref, own_rows) = refs[:HOLD], refs[HOLD:]
    fill_bias(reach_ref, kv_refs, bias_ref)
    own_rows[...] = own_ref[...].astype(F32)
    own_keys = [own_part(own_rows, g) for g in range(G)]
    own_values = [own_part(own_rows, G + g) for g in range(G)]
    scale = LOG2E / math.sqrt(D)
    for tile in range(TILES):
        seen = own_seen(tile)
        outs, lse = [], []
        for g in range(G):
            q = tile_queries(q_ref, tile, g)
            scores = block_scores(q, kv_refs, g, bias_ref)
            so = lax.dot_general(own_keys[g], q, CONTRACT_LAST, preferred_element_type=F32)
            so = jnp.where(seen, so, LOWEST)
            top = jnp.maximum(top_of(scores), jnp.max(so, axis=0, keepdims=True))
            values = block_values(kv_refs, g) + [own_values[g]]
            total, summed = weigh(scores + [so], values, top)
            summed = summed * (1.0 / total)
            outs.append(jnp.transpose(summed).reshape(SOURCES, ROWS, D))
            lse.append(top * scale + jnp.log2(total))
        finish(outs, lse, tile, out_ref)


def combine_kernel(lengths_ref, order_ref, in_ref, out_ref, rows_ref):
    lane = lax.broadcasted_iota(jnp.int32, (1, ROWS, D), 2)
    row = lax.broadcasted_iota(jnp.int32, (1, ROWS, D), 1)
    for h in range(HEADS):
        parts = [in_ref[:, h, g].astype(F32) for g in range(G)]
        stats = parts[0][:, LIVE : LIVE + 1, :]
        for g in range(G):
            mine = False
            for i in range(3):
                mine = mine | (lane == (g * 3 + i) * LIVE + row)
            mine = mine & (row < LIVE)
            lse = jnp.sum(jnp.where(mine, stats, 0.0), axis=2, keepdims=True)
            top = jnp.max(lse, axis=0, keepdims=True)
            w = jnp.exp2(lse - top)
            o = jnp.sum(parts[g] * w, axis=0) / jnp.sum(w, axis=0)
            at = (h * G + g) * ROWS
            rows_ref[at : at + ROWS, :] = jnp.where(row[0] < LIVE, o, 0.0)
    rows = jnp.dot(order_ref[...], rows_ref[...].astype(BF16), preferred_element_type=F32)
    heads = HEADS * G * J
    first = T * (ctx_of((0, 0)) * HEADS + lax.axis_index("xl") * C + lax.axis_index("c"))
    for t in range(T):
        for r in range(R):
            at = (t * R + r) * heads
            live = first + t < lengths_ref[r]
            out_ref[t, r] = jnp.where(live, rows[at : at + heads, :], 0.0).astype(BF16)


def message_order():
    order = np.zeros((MESSAGE, QUERIES), np.float32)
    for h in range(HEADS):
        for g in range(G):
            for r in range(R):
                for t in range(T):
                    for j in range(J):
                        to = (h * G + g) * ROWS + (r * T + t) * J + j
                        order[to, (t * R + r) * HEADS * G * J + (h * G + g) * J + j] = 1
    return order


def own_order():
    kv_heads = HEADS * G
    order = np.zeros((2 * T * R * kv_heads, 2 * T * R * kv_heads), np.float32)
    for h in range(HEADS):
        for kv in range(2):
            for g in range(G):
                for r in range(R):
                    for t in range(T):
                        to = ((h * 2 + kv) * G + g) * R * T + r * T + t
                        order[to, (kv * T * R + t * R + r) * kv_heads + h * G + g] = 1
    return order


def message_kernel(order_ref, own_order_ref, q_ref, k_ref, v_ref, message_ref, own_ref):
    q = q_ref[...].astype(F32).reshape(QUERIES, D).astype(BF16)
    rows = jnp.dot(order_ref[...], q, preferred_element_type=F32).astype(BF16)
    for z in range(Z):
        message_ref[z] = rows
    own = [ref[...].astype(F32).reshape(T * R * HEADS * G, D) for ref in (k_ref, v_ref)]
    own = jnp.concatenate(own, axis=0).astype(BF16)
    own = jnp.dot(own_order_ref[...], own, preferred_element_type=F32).astype(BF16)
    for hold in range(HOLD):
        own_ref[hold] = own


def pack_kernel(mask_ref, k_ref, v_ref, pack_ref, wide, mask_rows):
    for kv, ref in enumerate((k_ref, v_ref)):
        wide[kv] = ref[...].astype(F32)
        for g in range(G):
            at = (g * 2 + kv) * BLOCK
            pack_ref[at : at + BLOCK, :] = wide[kv, pl.ds(g, BLOCK, stride=G), :].astype(BF16)
    mask_rows[...] = jnp.zeros_like(mask_rows)
    mask_rows[0 : BLOCK // D, :] = mask_ref[...].astype(F32)
    pack_ref[MASK:PACK, :] = mask_rows[...].astype(BF16)


def permute(x, axis, size, shift):
    return lax.ppermute(x, axis, [(i, (i + shift) % size) for i in range(size)])


def per_device(
    prompt_keys,
    prompt_values,
    prompt_mask,
    response_queries,
    response_keys,
    response_values,
    resp_lengths,
    prompt_reach,
):
    plane = ("z", "xl", "c")
    near = ("y", "xh", "xl", "c")
    smem = pl.BlockSpec(memory_space=pltpu.SMEM)
    vmem = pl.BlockSpec(memory_space=pltpu.VMEM)
    order = message_order()
    kv = pl.pallas_call(
        pack_kernel,
        out_shape=jax.ShapeDtypeStruct((PACK, D), BF16),
        in_specs=[vmem] * 3,
        out_specs=vmem,
        scratch_shapes=[pltpu.VMEM((2, G * BLOCK, D), F32), pltpu.VMEM((16, D), F32)],
        name="pack",
    )(
        prompt_mask.reshape(BLOCK // D, D),
        prompt_keys.reshape(BLOCK * G, D),
        prompt_values.reshape(BLOCK * G, D),
    )
    across = permute(kv, "xh", XH, 1)
    far = permute(kv, "y", Y, 2)
    before = permute(kv, "y", Y, 1)
    after = permute(kv, "y", Y, 3)
    message, own = pl.pallas_call(
        message_kernel,
        out_shape=[
            jax.ShapeDtypeStruct((Z, MESSAGE, D), BF16),
            jax.ShapeDtypeStruct((HOLD, HEADS * OWN_PART, D), BF16),
        ],
        in_specs=[vmem] * 5,
        out_specs=[vmem] * 2,
        name="message",
    )(
        jnp.asarray(order, BF16),
        jnp.asarray(own_order(), BF16),
        response_queries,
        response_keys,
        response_values,
    )
    rows = lax.all_to_all(message.reshape(PLANE, G * ROWS, D), plane, 0, 0, tiled=True)
    rows, own = lax.optimization_barrier((rows, own))
    own = lax.all_to_all(own.reshape(NEAR, OWN_PART, D), near, 0, 0, tiled=True)
    across_before = permute(across, "y", Y, 1)
    across_after = permute(across, "y", Y, 3)
    across_far = permute(far, "xh", XH, 1)
    blocks = (kv, before, after, far, across, across_before, across_after, across_far)
    pair_flops = 4 * PLANE * G * ROWS * BLOCK * D
    partial = pl.pallas_call(
        attend_kernel,
        out_shape=jax.ShapeDtypeStruct((PLANE, G, ROWS, D), BF16),
        in_specs=[smem] + [vmem] * (2 + HOLD),
        out_specs=vmem,
        scratch_shapes=[
            pltpu.VMEM((HOLD, BLOCK, TILE), F32),
            pltpu.VMEM((NEAR * OWN_PART, D), F32),
        ],
        compiler_params=pltpu.CompilerParams(vmem_limit_bytes=32 << 20),
        cost_estimate=pl.CostEstimate(
            flops=9 * pair_flops, bytes_accessed=4 << 20, transcendentals=9 * pair_flops // 512
        ),
        name="attend",
    )(prompt_reach, rows.reshape(PLANE, G, ROWS, D), own.reshape(NEAR * OWN_PART, D), *blocks)
    partial = lax.all_to_all(partial.reshape(PLANE, G * ROWS, D), plane, 0, 0, tiled=True)
    return pl.pallas_call(
        combine_kernel,
        out_shape=jax.ShapeDtypeStruct((T, R, HEADS * G * J, D), BF16),
        in_specs=[smem, vmem, vmem],
        out_specs=vmem,
        scratch_shapes=[pltpu.VMEM((MESSAGE, D), F32)],
        name="combine",
    )(resp_lengths, jnp.asarray(order.T, BF16), partial.reshape(Z, HEADS, G, ROWS, D))


def solution(mesh):
    fine = Mesh(mesh.devices.reshape(Z, Y, XH, XL, C), ("z", "y", "xh", "xl", "c"))
    ctx, head = ("z", "y", "xh"), ("xl", "c")
    return jax.shard_map(
        per_device,
        mesh=fine,
        in_specs=(
            P(ctx, head, None),
            P(ctx, head, None),
            P(ctx),
            P(ctx + head, None, None, None),
            P(ctx + head, None, None, None),
            P(ctx + head, None, None, None),
            P(),
            P(),
        ),
        out_specs=P(ctx + head, None, None, None),
        check_vma=False,
    )
```

```python
import functools
import math

import jax
import jax.numpy as jnp
import numpy as np
from jax import lax
from jax.experimental import pallas as pl
from jax.experimental.pallas import tpu as pltpu
from jax.sharding import Mesh, PartitionSpec as P

ZZ, ZC, Y, XH, XL, C = 4, 2, 4, 2, 2, 2
HEADS = XL * C
SPREAD = ZZ * ZC
PLANE = SPREAD * HEADS
HOLD = Y * XH
T, R, G, J, D = 2, 2, 2, 5, 128
LIVE = R * T * J
ROWS = 24
BLOCK = 256
QUERIES = T * R * HEADS * G * J
MESSAGE = HEADS * G * ROWS
MASK = 4 * BLOCK
OWN = MASK + 16
OWN_ROWS = HEADS * R * T
PACK = OWN + 2 * G * OWN_ROWS
OWN_PART = 2 * G * R * T
BLOCKS = ((0, 0), (3, 0), (1, 0), (2, 0), (0, 1), (3, 1), (1, 1), (2, 1))
SOURCES = 16
TILE = SOURCES * ROWS
TILES = PLANE // SOURCES
LOWEST = -1e30
HIDE_FLOPS = int(3 * (1 << 30))
LOG2E = math.log2(math.e)
F32 = jnp.float32
BF16 = jnp.bfloat16
CONTRACT_LAST = (((1,), (1,)), ((), ()))


def three_parts(x):
    hi = x.astype(BF16).astype(F32)
    mid = (x - hi).astype(BF16).astype(F32)
    lo = (x - hi - mid).astype(BF16).astype(F32)
    return hi, mid, lo


def device_of(zz, zc, y, xh, head):
    return (((zz * ZC + zc) * Y + y) * XH + xh) * HEADS + head


def place_of(offset):
    dy, dxh = offset
    y = lax.rem(lax.axis_index("y") + dy, Y)
    xh = lax.rem(lax.axis_index("xh") + dxh, XH)
    return device_of(lax.axis_index("zz"), lax.axis_index("zc"), y, xh, 0) // HEADS * BLOCK


def row_parts():
    lane = lax.broadcasted_iota(jnp.int32, (1, TILE), 1)
    source = (lane * 2731) >> 16
    return source, lane - source * ROWS


def hide_kernel(reach_ref, *refs):
    kv_refs, hide_ref = refs[:HOLD], refs[HOLD]
    lane = lax.broadcasted_iota(jnp.int32, (1, D), 1)
    sub = lax.broadcasted_iota(jnp.int32, (8, D), 0)
    reach = jnp.where(sub == 0, reach_ref[0], reach_ref[1])
    for b, (kv_ref, offset) in enumerate(zip(kv_refs, BLOCKS)):
        first = place_of(offset)
        mask = kv_ref[...].astype(F32)
        for i in range(BLOCK // D):
            seen = (mask[i : i + 1, :] > 0.5) & (first + i * D + lane < reach)
            hide_ref[b, :, i * D : (i + 1) * D] = jnp.where(seen, 0.0, LOWEST)


def fill_bias(hide_ref, bias_ref):
    _, within = row_parts()
    row_r = jnp.where(within >= T * J, 1, 0)
    pick = (lax.broadcasted_iota(jnp.int32, (8, TILE), 0) == row_r).astype(F32).astype(BF16)
    for b in range(HOLD):
        bias_ref[b] = lax.dot_general(
            hide_ref[b].astype(BF16), pick, (((0,), (0,)), ((), ())), preferred_element_type=F32
        )


def tile_queries(q_ref, tile, g):
    q = q_ref[tile * SOURCES : (tile + 1) * SOURCES, g].astype(F32)
    return q.reshape(TILE, D).astype(BF16)


def block_scores(q, kv_refs, g, bias_ref):
    scores = []
    for b, kv_ref in enumerate(kv_refs):
        keys = kv_ref[g * 2 * BLOCK : g * 2 * BLOCK + BLOCK, :]
        s = lax.dot_general(keys, q, CONTRACT_LAST, preferred_element_type=F32)
        scores.append(s + bias_ref[b])
    return scores


def block_values(kv_refs, g):
    return [kv_ref[g * 2 * BLOCK + BLOCK : (g + 1) * 2 * BLOCK, :] for kv_ref in kv_refs]


def weigh(scores, values, top):
    scale = LOG2E / math.sqrt(D)
    total, summed = 0.0, 0.0
    top = top * scale
    for s, v in zip(scores, values):
        p = jnp.exp2(s * scale - top)
        total = total + jnp.sum(p, axis=0, keepdims=True)
        summed = summed + lax.dot_general(
            v, p.astype(BF16), (((0,), (0,)), ((), ())), preferred_element_type=F32
        )
    return total, summed


def top_of(scores):
    wide = functools.reduce(jnp.maximum, scores)
    return jnp.max(wide, axis=0, keepdims=True)


def finish(outs, lse, tile, out_ref):
    source, within = row_parts()
    mine = lax.broadcasted_iota(jnp.int32, (SOURCES, TILE), 0) == source
    row = lax.broadcasted_iota(jnp.int32, (SOURCES, ROWS, D), 1).reshape(TILE, D)
    lane = lax.broadcasted_iota(jnp.int32, (TILE, D), 1)
    spread = ((row == lane) & (row < LIVE)).astype(F32).astype(BF16)
    stats = 0.0
    for g in range(G):
        for i, part in enumerate(three_parts(lse[g])):
            rows = jnp.where(mine, part, 0.0).astype(BF16)
            rows = jnp.dot(rows, spread, preferred_element_type=F32)
            at = (g * 3 + i) * LIVE
            stats = stats + (pltpu.roll(rows, at, 1) if at else rows)
    at = slice(tile * SOURCES, (tile + 1) * SOURCES)
    spare = lax.broadcasted_iota(jnp.int32, (SOURCES, ROWS, D), 1) == LIVE
    out_ref[at, 0] = jnp.where(spare, stats[:, None, :], outs[0]).astype(BF16)
    out_ref[at, 1] = outs[1].astype(BF16)


def own_seen(tile):
    source, within = row_parts()
    is_r1 = within >= T * J
    in_r = jnp.where(is_r1, within - T * J, within)
    row_r = jnp.where(is_r1, 1, 0)
    row_t = jnp.where(in_r >= J, 1, 0)
    k = lax.broadcasted_iota(jnp.int32, (HOLD * OWN_ROWS, 1), 0)
    own_place = T * ((k >> 2) & 3) + (k & 1)
    for b, offset in enumerate(BLOCKS):
        first = place_of(offset) // BLOCK * HEADS * T
        own_place = own_place + jnp.where((k >> 4) == b, first, 0)
    own_r = (k >> 1) & 1
    zz, zc, y, xh = (lax.axis_index(name) for name in ("zz", "zc", "y", "xh"))
    from_source = tile * SOURCES + source
    row_device = device_of(from_source >> 3, (from_source >> 2) & 1, y, xh, from_source & 3)
    row_place = T * row_device + row_t
    return (own_r == row_r) & (own_place <= row_place)


def own_part(kv_refs, kind):
    at = OWN + kind * OWN_ROWS
    return jnp.concatenate([ref[at : at + OWN_ROWS, :] for ref in kv_refs], axis=0)


def attend_kernel(hide_ref, q_ref, *refs):
    kv_refs, (out_ref, bias_ref) = refs[:HOLD], refs[HOLD:]
    fill_bias(hide_ref, bias_ref)
    own_keys = [own_part(kv_refs, g) for g in range(G)]
    own_values = [own_part(kv_refs, G + g) for g in range(G)]
    scale = LOG2E / math.sqrt(D)
    for tile in range(TILES):
        seen = own_seen(tile)
        outs, lse = [], []
        for g in range(G):
            q = tile_queries(q_ref, tile, g)
            scores = block_scores(q, kv_refs, g, bias_ref)
            so = lax.dot_general(own_keys[g], q, CONTRACT_LAST, preferred_element_type=F32)
            so = jnp.where(seen, so, LOWEST)
            top = jnp.maximum(top_of(scores), jnp.max(so, axis=0, keepdims=True))
            values = block_values(kv_refs, g) + [own_values[g]]
            total, summed = weigh(scores + [so], values, top)
            summed = summed * (1.0 / total)
            outs.append(jnp.transpose(summed).reshape(SOURCES, ROWS, D))
            lse.append(top * scale + jnp.log2(total))
        finish(outs, lse, tile, out_ref)


def combine_kernel(lengths_ref, order_ref, in_ref, out_ref, rows_ref):
    lane = lax.broadcasted_iota(jnp.int32, (1, ROWS, D), 2)
    row = lax.broadcasted_iota(jnp.int32, (1, ROWS, D), 1)
    for h in range(HEADS):
        parts = [in_ref[:, h, g].astype(F32) for g in range(G)]
        stats = parts[0][:, LIVE : LIVE + 1, :]
        for g in range(G):
            mine = False
            for i in range(3):
                mine = mine | (lane == (g * 3 + i) * LIVE + row)
            mine = mine & (row < LIVE)
            lse = jnp.sum(jnp.where(mine, stats, 0.0), axis=2, keepdims=True)
            top = jnp.max(lse, axis=0, keepdims=True)
            w = jnp.exp2(lse - top)
            o = jnp.sum(parts[g] * w, axis=0) / jnp.sum(w, axis=0)
            at = (h * G + g) * ROWS
            rows_ref[at : at + ROWS, :] = jnp.where(row[0] < LIVE, o, 0.0)
    rows = jnp.dot(order_ref[...], rows_ref[...].astype(BF16), preferred_element_type=F32)
    heads = HEADS * G * J
    names = ("zz", "zc", "y", "xh")
    head = lax.axis_index("xl") * C + lax.axis_index("c")
    first = T * device_of(*(lax.axis_index(name) for name in names), head)
    for t in range(T):
        for r in range(R):
            at = (t * R + r) * heads
            live = first + t < lengths_ref[r]
            out_ref[t, r] = jnp.where(live, rows[at : at + heads, :], 0.0).astype(BF16)


def message_order():
    order = np.zeros((MESSAGE, QUERIES), np.float32)
    for h in range(HEADS):
        for g in range(G):
            for r in range(R):
                for t in range(T):
                    for j in range(J):
                        to = (h * G + g) * ROWS + (r * T + t) * J + j
                        order[to, (t * R + r) * HEADS * G * J + (h * G + g) * J + j] = 1
    return order


def own_order():
    kv_heads = HEADS * G
    order = np.zeros((2 * T * R * kv_heads, 2 * T * R * kv_heads), np.float32)
    for h in range(HEADS):
        for kv in range(2):
            for g in range(G):
                for r in range(R):
                    for t in range(T):
                        to = ((h * 2 + kv) * G + g) * R * T + r * T + t
                        order[to, (kv * T * R + t * R + r) * kv_heads + h * G + g] = 1
    return order


def own_kernel(own_order_ref, k_ref, v_ref, *refs):
    own_refs, own_rows = refs[:HEADS], refs[HEADS]
    own = [ref[...].astype(F32).reshape(T * R * HEADS * G, D) for ref in (k_ref, v_ref)]
    own = jnp.concatenate(own, axis=0).astype(BF16)
    own = jnp.dot(own_order_ref[...], own, preferred_element_type=F32)
    own_rows[...] = own.reshape(HEADS, OWN_PART, D)
    head = lax.axis_index("xl") * C + lax.axis_index("c")
    for step, own_ref in enumerate(own_refs):
        own_ref[...] = own_rows[lax.rem(head + step, HEADS)].astype(BF16)


def message_kernel(order_ref, q_ref, message_ref):
    q = q_ref[...].astype(F32).reshape(QUERIES, D).astype(BF16)
    rows = jnp.dot(order_ref[...], q, preferred_element_type=F32).astype(BF16)
    for to in range(SPREAD):
        message_ref[to] = rows


def pack_kernel(mask_ref, k_ref, v_ref, *refs):
    own_refs, (pack_ref, wide, by_head, sorted_rows) = refs[:HEADS], refs[HEADS:]
    for kv, ref in enumerate((k_ref, v_ref)):
        wide[kv] = ref[...].astype(F32)
        for g in range(G):
            at = (g * 2 + kv) * BLOCK
            pack_ref[at : at + BLOCK, :] = wide[kv, pl.ds(g, BLOCK, stride=G), :].astype(BF16)
    head = lax.axis_index("xl") * C + lax.axis_index("c")
    for step, own_ref in enumerate(own_refs):
        by_head[lax.rem(head + HEADS - step, HEADS)] = own_ref[...].astype(F32)
    part = T * R
    for h in range(HEADS):
        for kind in range(2 * G):
            at = kind * OWN_ROWS + h * part
            sorted_rows[at : at + part, :] = by_head[h, kind * part : (kind + 1) * part, :]
    pack_ref[OWN:PACK, :] = sorted_rows[...].astype(BF16)
    by_head[0] = jnp.zeros((OWN_PART, D), F32)
    by_head[0, 0 : BLOCK // D, :] = mask_ref[...].astype(F32)
    pack_ref[MASK:OWN, :] = by_head[0].astype(BF16)


def permute(x, axis, size, shift):
    return lax.ppermute(x, axis, [(i, (i + shift) % size) for i in range(size)])


def per_device(
    prompt_keys,
    prompt_values,
    prompt_mask,
    response_queries,
    response_keys,
    response_values,
    resp_lengths,
    prompt_reach,
):
    plane = ("zz", "zc", "xl", "c")
    smem = pl.BlockSpec(memory_space=pltpu.SMEM)
    vmem = pl.BlockSpec(memory_space=pltpu.VMEM)
    order = message_order()
    own = pl.pallas_call(
        own_kernel,
        out_shape=[jax.ShapeDtypeStruct((OWN_PART, D), BF16)] * HEADS,
        in_specs=[vmem] * 3,
        out_specs=[vmem] * HEADS,
        scratch_shapes=[pltpu.VMEM((HEADS, OWN_PART, D), F32)],
        name="own",
    )(jnp.asarray(own_order(), BF16), response_keys, response_values)
    own = [own[0]] + [permute(own[step], ("xl", "c"), HEADS, step) for step in range(1, HEADS)]
    message = pl.pallas_call(
        message_kernel,
        out_shape=jax.ShapeDtypeStruct((SPREAD, MESSAGE, D), BF16),
        in_specs=[vmem] * 2,
        out_specs=vmem,
        name="message",
    )(jnp.asarray(order, BF16), response_queries)
    kv = pl.pallas_call(
        pack_kernel,
        out_shape=jax.ShapeDtypeStruct((PACK, D), BF16),
        in_specs=[vmem] * (3 + HEADS),
        out_specs=vmem,
        scratch_shapes=[
            pltpu.VMEM((2, G * BLOCK, D), F32),
            pltpu.VMEM((HEADS, OWN_PART, D), F32),
            pltpu.VMEM((HEADS * OWN_PART, D), F32),
        ],
        name="pack",
    )(
        prompt_mask.reshape(BLOCK // D, D),
        prompt_keys.reshape(BLOCK * G, D),
        prompt_values.reshape(BLOCK * G, D),
        *own,
    )
    message, kv = lax.optimization_barrier((message, kv))
    across = permute(kv, "xh", XH, 1)
    far = permute(kv, "y", Y, 2)
    before = permute(kv, "y", Y, 1)
    after = permute(kv, "y", Y, 3)
    rows = lax.all_to_all(message.reshape(PLANE, G * ROWS, D), plane, 0, 0, tiled=True)
    across_before = permute(across, "y", Y, 1)
    across_after = permute(across, "y", Y, 3)
    across_far = permute(far, "xh", XH, 1)
    blocks = (kv, before, after, far, across, across_before, across_after, across_far)
    hide = pl.pallas_call(
        hide_kernel,
        out_shape=jax.ShapeDtypeStruct((HOLD, 8, BLOCK), F32),
        grid=(1,),
        in_specs=[smem] + [pl.BlockSpec((OWN - MASK, D), lambda i: (MASK // 16, 0))] * HOLD,
        out_specs=pl.BlockSpec((HOLD, 8, BLOCK), lambda i: (0, 0, 0)),
        compiler_params=pltpu.CompilerParams(vmem_limit_bytes=4 << 20),
        cost_estimate=pl.CostEstimate(flops=HIDE_FLOPS, bytes_accessed=1 << 20, transcendentals=0),
        name="hide",
    )(prompt_reach, *blocks)
    pair_flops = 4 * PLANE * G * ROWS * BLOCK * D
    partial = pl.pallas_call(
        attend_kernel,
        out_shape=jax.ShapeDtypeStruct((PLANE, G, ROWS, D), BF16),
        in_specs=[vmem] * (2 + HOLD),
        out_specs=vmem,
        scratch_shapes=[pltpu.VMEM((HOLD, BLOCK, TILE), F32)],
        compiler_params=pltpu.CompilerParams(vmem_limit_bytes=32 << 20),
        cost_estimate=pl.CostEstimate(
            flops=9 * pair_flops, bytes_accessed=4 << 20, transcendentals=9 * pair_flops // 512
        ),
        name="attend",
    )(hide, rows.reshape(PLANE, G, ROWS, D), *blocks)
    partial = lax.all_to_all(partial.reshape(PLANE, G * ROWS, D), plane, 0, 0, tiled=True)
    return pl.pallas_call(
        combine_kernel,
        out_shape=jax.ShapeDtypeStruct((T, R, HEADS * G * J, D), BF16),
        in_specs=[smem, vmem, vmem],
        out_specs=vmem,
        scratch_shapes=[pltpu.VMEM((MESSAGE, D), F32)],
        name="combine",
    )(resp_lengths, jnp.asarray(order.T, BF16), partial.reshape(SPREAD, HEADS, G, ROWS, D))


def solution(mesh):
    names = ("zz", "zc", "y", "xh", "xl", "c")
    fine = Mesh(mesh.devices.reshape(ZZ, ZC, Y, XH, XL, C), names)
    ctx, head = names[:4], names[4:]
    return jax.shard_map(
        per_device,
        mesh=fine,
        in_specs=(
            P(ctx, head, None),
            P(ctx, head, None),
            P(ctx),
            P(ctx + head, None, None, None),
            P(ctx + head, None, None, None),
            P(ctx + head, None, None, None),
            P(),
            P(),
        ),
        out_specs=P(ctx + head, None, None, None),
        check_vma=False,
    )
```

```python
import functools
import math

import jax
import jax.numpy as jnp
import numpy as np
from jax import lax
from jax.experimental import pallas as pl
from jax.experimental.pallas import tpu as pltpu
from jax.sharding import Mesh, PartitionSpec as P

ZZ, ZC, Y, XH, XL, C = 4, 2, 4, 2, 2, 2
HEADS = XL * C
SPREAD = ZZ * ZC
PLANE = SPREAD * HEADS
HOLD = Y * XH
T, R, G, J, D = 2, 2, 2, 5, 128
LIVE = R * T * J
ROWS = 24
BLOCK = 256
QUERIES = T * R * HEADS * G * J
MESSAGE = HEADS * G * ROWS
MASK = 4 * BLOCK
OWN = MASK + 16
OWN_ROWS = HEADS * R * T
PACK = OWN + 2 * G * OWN_ROWS
OWN_PART = 2 * G * R * T
BLOCKS = ((0, 0), (3, 0), (1, 0), (2, 0), (0, 1), (3, 1), (1, 1), (2, 1))
SOURCES = 16
TILE = SOURCES * ROWS
TILES = PLANE // SOURCES
LOWEST = -1e30
HIDE_FLOPS = int(6 * (1 << 30))
FIRST_FLOPS = int(1 * (1 << 30))
EARLY = 5
LOG2E = math.log2(math.e)
F32 = jnp.float32
BF16 = jnp.bfloat16
CONTRACT_LAST = (((1,), (1,)), ((), ()))


def three_parts(x):
    hi = x.astype(BF16).astype(F32)
    mid = (x - hi).astype(BF16).astype(F32)
    lo = (x - hi - mid).astype(BF16).astype(F32)
    return hi, mid, lo


def device_of(zz, zc, y, xh, head):
    return (((zz * ZC + zc) * Y + y) * XH + xh) * HEADS + head


def place_of(offset):
    dy, dxh = offset
    y = lax.rem(lax.axis_index("y") + dy, Y)
    xh = lax.rem(lax.axis_index("xh") + dxh, XH)
    return device_of(lax.axis_index("zz"), lax.axis_index("zc"), y, xh, 0) // HEADS * BLOCK


def row_parts():
    lane = lax.broadcasted_iota(jnp.int32, (1, TILE), 1)
    source = (lane * 2731) >> 16
    return source, lane - source * ROWS


def hide_rows(reach_ref, mask, offset):
    lane = lax.broadcasted_iota(jnp.int32, (1, D), 1)
    sub = lax.broadcasted_iota(jnp.int32, (8, D), 0)
    reach = jnp.where(sub == 0, reach_ref[0], reach_ref[1])
    first = place_of(offset)
    parts = []
    for i in range(BLOCK // D):
        seen = (mask[i : i + 1, :] > 0.5) & (first + i * D + lane < reach)
        parts.append(jnp.where(seen, 0.0, LOWEST))
    return jnp.concatenate(parts, axis=1)


def hide_kernel(reach_ref, *refs):
    mask_refs, hide_ref = refs[:-1], refs[-1]
    for b, mask_ref in enumerate(mask_refs):
        hide_ref[b] = hide_rows(reach_ref, mask_ref[...].astype(F32), BLOCKS[b])


def bias_of(hide):
    _, within = row_parts()
    row_r = jnp.where(within >= T * J, 1, 0)
    pick = (lax.broadcasted_iota(jnp.int32, (8, TILE), 0) == row_r).astype(F32).astype(BF16)
    return lax.dot_general(
        hide.astype(BF16), pick, (((0,), (0,)), ((), ())), preferred_element_type=F32
    )


def tile_queries(q_ref, tile, g):
    q = q_ref[tile * SOURCES : (tile + 1) * SOURCES, g].astype(F32)
    return q.reshape(TILE, D).astype(BF16)


def block_scores(q, kv_refs, g, bias_ref):
    scores = []
    for b, kv_ref in enumerate(kv_refs):
        keys = kv_ref[g * 2 * BLOCK : g * 2 * BLOCK + BLOCK, :]
        s = lax.dot_general(keys, q, CONTRACT_LAST, preferred_element_type=F32)
        scores.append(s + bias_ref[b])
    return scores


def block_values(kv_refs, g):
    return [kv_ref[g * 2 * BLOCK + BLOCK : (g + 1) * 2 * BLOCK, :] for kv_ref in kv_refs]


def weigh(scores, values, top):
    scale = LOG2E / math.sqrt(D)
    total, summed = 0.0, 0.0
    top = top * scale
    for s, v in zip(scores, values):
        p = jnp.exp2(s * scale - top)
        total = total + jnp.sum(p, axis=0, keepdims=True)
        summed = summed + lax.dot_general(
            v, p.astype(BF16), (((0,), (0,)), ((), ())), preferred_element_type=F32
        )
    return total, summed


def top_of(scores):
    wide = functools.reduce(jnp.maximum, scores)
    return jnp.max(wide, axis=0, keepdims=True)


def finish(outs, lse, tile, out_ref):
    source, within = row_parts()
    mine = lax.broadcasted_iota(jnp.int32, (SOURCES, TILE), 0) == source
    row = lax.broadcasted_iota(jnp.int32, (SOURCES, ROWS, D), 1).reshape(TILE, D)
    lane = lax.broadcasted_iota(jnp.int32, (TILE, D), 1)
    spread = ((row == lane) & (row < LIVE)).astype(F32).astype(BF16)
    stats = 0.0
    for g in range(G):
        for i, part in enumerate(three_parts(lse[g])):
            rows = jnp.where(mine, part, 0.0).astype(BF16)
            rows = jnp.dot(rows, spread, preferred_element_type=F32)
            at = (g * 3 + i) * LIVE
            stats = stats + (pltpu.roll(rows, at, 1) if at else rows)
    at = slice(tile * SOURCES, (tile + 1) * SOURCES)
    spare = lax.broadcasted_iota(jnp.int32, (SOURCES, ROWS, D), 1) == LIVE
    out_ref[at, 0] = jnp.where(spare, stats[:, None, :], outs[0]).astype(BF16)
    out_ref[at, 1] = outs[1].astype(BF16)


def own_seen(tile):
    source, within = row_parts()
    is_r1 = within >= T * J
    in_r = jnp.where(is_r1, within - T * J, within)
    row_r = jnp.where(is_r1, 1, 0)
    row_t = jnp.where(in_r >= J, 1, 0)
    k = lax.broadcasted_iota(jnp.int32, (HOLD * OWN_ROWS, 1), 0)
    own_place = T * ((k >> 2) & 3) + (k & 1)
    for b, offset in enumerate(BLOCKS):
        first = place_of(offset) // BLOCK * HEADS * T
        own_place = own_place + jnp.where((k >> 4) == b, first, 0)
    own_r = (k >> 1) & 1
    zz, zc, y, xh = (lax.axis_index(name) for name in ("zz", "zc", "y", "xh"))
    from_source = tile * SOURCES + source
    row_device = device_of(from_source >> 3, (from_source >> 2) & 1, y, xh, from_source & 3)
    row_place = T * row_device + row_t
    return (own_r == row_r) & (own_place <= row_place)


def own_part(kv_refs, kind):
    at = OWN + kind * OWN_ROWS
    return jnp.concatenate([ref[at : at + OWN_ROWS, :] for ref in kv_refs], axis=0)


def first_kernel(hide_ref, q_ref, *refs):
    kv_refs, (acc_ref, stat_ref, bias_ref) = refs[:EARLY], refs[EARLY:]
    for b in range(EARLY):
        bias_ref[b] = bias_of(hide_ref[b])
    for g in range(G):
        for tile in range(TILES):
            q = tile_queries(q_ref, tile, g)
            scores = block_scores(q, kv_refs, g, bias_ref)
            top = top_of(scores)
            total, summed = weigh(scores, block_values(kv_refs, g), top)
            acc_ref[tile, g] = summed
            stat_ref[tile, g, 0:1, :] = top
            stat_ref[tile, g, 1:2, :] = total


def second_kernel(reach_ref, q_ref, *refs):
    all_refs, (acc_ref, stat_ref, out_ref, bias_ref) = refs[:HOLD], refs[HOLD:]
    kv_refs = all_refs[EARLY:]
    for b, kv_ref in enumerate(kv_refs):
        mask = kv_ref[MASK:OWN, :].astype(F32)
        bias_ref[b] = bias_of(hide_rows(reach_ref, mask, BLOCKS[EARLY + b]))
    own_keys = [own_part(all_refs, g) for g in range(G)]
    own_values = [own_part(all_refs, G + g) for g in range(G)]
    scale = LOG2E / math.sqrt(D)
    for tile in range(TILES):
        seen = own_seen(tile)
        outs, lse = [], []
        for g in range(G):
            q = tile_queries(q_ref, tile, g)
            scores = block_scores(q, kv_refs, g, bias_ref)
            so = lax.dot_general(own_keys[g], q, CONTRACT_LAST, preferred_element_type=F32)
            so = jnp.where(seen, so, LOWEST)
            before = stat_ref[tile, g]
            top_before, total_before = before[0:1, :], before[1:2, :]
            top = jnp.maximum(top_of(scores), jnp.max(so, axis=0, keepdims=True))
            top = jnp.maximum(top, top_before)
            values = block_values(kv_refs, g) + [own_values[g]]
            total, summed = weigh(scores + [so], values, top)
            shrink = jnp.exp2((top_before - top) * scale)
            total = total + total_before * shrink
            summed = (summed + acc_ref[tile, g] * shrink) * (1.0 / total)
            outs.append(jnp.transpose(summed).reshape(SOURCES, ROWS, D))
            lse.append(top * scale + jnp.log2(total))
        finish(outs, lse, tile, out_ref)


def combine_kernel(lengths_ref, order_ref, in_ref, out_ref, rows_ref):
    lane = lax.broadcasted_iota(jnp.int32, (1, ROWS, D), 2)
    row = lax.broadcasted_iota(jnp.int32, (1, ROWS, D), 1)
    for h in range(HEADS):
        parts = [in_ref[:, h, g].astype(F32) for g in range(G)]
        stats = parts[0][:, LIVE : LIVE + 1, :]
        for g in range(G):
            mine = False
            for i in range(3):
                mine = mine | (lane == (g * 3 + i) * LIVE + row)
            mine = mine & (row < LIVE)
            lse = jnp.sum(jnp.where(mine, stats, 0.0), axis=2, keepdims=True)
            top = jnp.max(lse, axis=0, keepdims=True)
            w = jnp.exp2(lse - top)
            o = jnp.sum(parts[g] * w, axis=0) / jnp.sum(w, axis=0)
            at = (h * G + g) * ROWS
            rows_ref[at : at + ROWS, :] = jnp.where(row[0] < LIVE, o, 0.0)
    rows = jnp.dot(order_ref[...], rows_ref[...].astype(BF16), preferred_element_type=F32)
    heads = HEADS * G * J
    names = ("zz", "zc", "y", "xh")
    head = lax.axis_index("xl") * C + lax.axis_index("c")
    first = T * device_of(*(lax.axis_index(name) for name in names), head)
    for t in range(T):
        for r in range(R):
            at = (t * R + r) * heads
            live = first + t < lengths_ref[r]
            out_ref[t, r] = jnp.where(live, rows[at : at + heads, :], 0.0).astype(BF16)


def message_order():
    order = np.zeros((MESSAGE, QUERIES), np.float32)
    for h in range(HEADS):
        for g in range(G):
            for r in range(R):
                for t in range(T):
                    for j in range(J):
                        to = (h * G + g) * ROWS + (r * T + t) * J + j
                        order[to, (t * R + r) * HEADS * G * J + (h * G + g) * J + j] = 1
    return order


def own_order():
    kv_heads = HEADS * G
    order = np.zeros((2 * T * R * kv_heads, 2 * T * R * kv_heads), np.float32)
    for h in range(HEADS):
        for kv in range(2):
            for g in range(G):
                for r in range(R):
                    for t in range(T):
                        to = ((h * 2 + kv) * G + g) * R * T + r * T + t
                        order[to, (kv * T * R + t * R + r) * kv_heads + h * G + g] = 1
    return order


def own_kernel(own_order_ref, k_ref, v_ref, *refs):
    own_refs, own_rows = refs[:HEADS], refs[HEADS]
    own = [ref[...].astype(F32).reshape(T * R * HEADS * G, D) for ref in (k_ref, v_ref)]
    own = jnp.concatenate(own, axis=0).astype(BF16)
    own = jnp.dot(own_order_ref[...], own, preferred_element_type=F32)
    own_rows[...] = own.reshape(HEADS, OWN_PART, D)
    head = lax.axis_index("xl") * C + lax.axis_index("c")
    for step, own_ref in enumerate(own_refs):
        own_ref[...] = own_rows[lax.rem(head + step, HEADS)].astype(BF16)


def message_kernel(order_ref, q_ref, message_ref):
    q = q_ref[...].astype(F32).reshape(QUERIES, D).astype(BF16)
    rows = jnp.dot(order_ref[...], q, preferred_element_type=F32).astype(BF16)
    for to in range(SPREAD):
        message_ref[to] = rows


def pack_kernel(mask_ref, k_ref, v_ref, *refs):
    own_refs, (pack_ref, wide, by_head, sorted_rows) = refs[:HEADS], refs[HEADS:]
    for kv, ref in enumerate((k_ref, v_ref)):
        wide[kv] = ref[...].astype(F32)
        for g in range(G):
            at = (g * 2 + kv) * BLOCK
            pack_ref[at : at + BLOCK, :] = wide[kv, pl.ds(g, BLOCK, stride=G), :].astype(BF16)
    head = lax.axis_index("xl") * C + lax.axis_index("c")
    for step, own_ref in enumerate(own_refs):
        by_head[lax.rem(head + HEADS - step, HEADS)] = own_ref[...].astype(F32)
    part = T * R
    for h in range(HEADS):
        for kind in range(2 * G):
            at = kind * OWN_ROWS + h * part
            sorted_rows[at : at + part, :] = by_head[h, kind * part : (kind + 1) * part, :]
    pack_ref[OWN:PACK, :] = sorted_rows[...].astype(BF16)
    by_head[0] = jnp.zeros((OWN_PART, D), F32)
    by_head[0, 0 : BLOCK // D, :] = mask_ref[...].astype(F32)
    pack_ref[MASK:OWN, :] = by_head[0].astype(BF16)


def permute(x, axis, size, shift):
    return lax.ppermute(x, axis, [(i, (i + shift) % size) for i in range(size)])


def per_device(
    prompt_keys,
    prompt_values,
    prompt_mask,
    response_queries,
    response_keys,
    response_values,
    resp_lengths,
    prompt_reach,
):
    plane = ("zz", "zc", "xl", "c")
    smem = pl.BlockSpec(memory_space=pltpu.SMEM)
    vmem = pl.BlockSpec(memory_space=pltpu.VMEM)
    order = message_order()
    own = pl.pallas_call(
        own_kernel,
        out_shape=[jax.ShapeDtypeStruct((OWN_PART, D), BF16)] * HEADS,
        in_specs=[vmem] * 3,
        out_specs=[vmem] * HEADS,
        scratch_shapes=[pltpu.VMEM((HEADS, OWN_PART, D), F32)],
        name="own",
    )(jnp.asarray(own_order(), BF16), response_keys, response_values)
    own = [own[0]] + [permute(own[step], ("xl", "c"), HEADS, step) for step in range(1, HEADS)]
    message = pl.pallas_call(
        message_kernel,
        out_shape=jax.ShapeDtypeStruct((SPREAD, MESSAGE, D), BF16),
        in_specs=[vmem] * 2,
        out_specs=vmem,
        name="message",
    )(jnp.asarray(order, BF16), response_queries)
    kv = pl.pallas_call(
        pack_kernel,
        out_shape=jax.ShapeDtypeStruct((PACK, D), BF16),
        in_specs=[vmem] * (3 + HEADS),
        out_specs=vmem,
        scratch_shapes=[
            pltpu.VMEM((2, G * BLOCK, D), F32),
            pltpu.VMEM((HEADS, OWN_PART, D), F32),
            pltpu.VMEM((HEADS * OWN_PART, D), F32),
        ],
        name="pack",
    )(
        prompt_mask.reshape(BLOCK // D, D),
        prompt_keys.reshape(BLOCK * G, D),
        prompt_values.reshape(BLOCK * G, D),
        *own,
    )
    message, kv = lax.optimization_barrier((message, kv))
    across = permute(kv, "xh", XH, 1)
    far = permute(kv, "y", Y, 2)
    before = permute(kv, "y", Y, 1)
    after = permute(kv, "y", Y, 3)
    rows = lax.all_to_all(message.reshape(PLANE, G * ROWS, D), plane, 0, 0, tiled=True)
    across_before = permute(across, "y", Y, 1)
    across_after = permute(across, "y", Y, 3)
    across_far = permute(far, "xh", XH, 1)
    blocks = (kv, before, after, far, across, across_before, across_after, across_far)
    hide = pl.pallas_call(
        hide_kernel,
        out_shape=jax.ShapeDtypeStruct((EARLY, 8, BLOCK), F32),
        grid=(1,),
        in_specs=[smem]
        + [pl.BlockSpec((OWN - MASK, D), lambda i: (MASK // 16, 0))] * (EARLY),
        out_specs=pl.BlockSpec((EARLY, 8, BLOCK), lambda i: (0, 0, 0)),
        compiler_params=pltpu.CompilerParams(vmem_limit_bytes=4 << 20),
        cost_estimate=pl.CostEstimate(flops=HIDE_FLOPS, bytes_accessed=1 << 20, transcendentals=0),
        name="hide",
    )(prompt_reach, *blocks[:EARLY])
    rows = rows.reshape(PLANE, G, ROWS, D)
    acc, stat = pl.pallas_call(
        first_kernel,
        out_shape=[
            jax.ShapeDtypeStruct((TILES, G, D, TILE), F32),
            jax.ShapeDtypeStruct((TILES, G, 8, TILE), F32),
        ],
        in_specs=[vmem] * (2 + EARLY),
        out_specs=[vmem] * 2,
        scratch_shapes=[pltpu.VMEM((EARLY, BLOCK, TILE), F32)],
        compiler_params=pltpu.CompilerParams(vmem_limit_bytes=24 << 20),
        cost_estimate=pl.CostEstimate(flops=FIRST_FLOPS, bytes_accessed=2 << 20, transcendentals=0),
        name="attend_first",
    )(hide, rows, *blocks[:EARLY])
    partial = pl.pallas_call(
        second_kernel,
        out_shape=jax.ShapeDtypeStruct((PLANE, G, ROWS, D), BF16),
        in_specs=[smem] + [vmem] * (3 + HOLD),
        out_specs=vmem,
        scratch_shapes=[pltpu.VMEM((HOLD - EARLY, BLOCK, TILE), F32)],
        compiler_params=pltpu.CompilerParams(vmem_limit_bytes=24 << 20),
        cost_estimate=pl.CostEstimate(flops=2 << 30, bytes_accessed=3 << 20, transcendentals=0),
        name="attend_second",
    )(prompt_reach, rows, *blocks, acc, stat)
    partial = lax.all_to_all(partial.reshape(PLANE, G * ROWS, D), plane, 0, 0, tiled=True)
    return pl.pallas_call(
        combine_kernel,
        out_shape=jax.ShapeDtypeStruct((T, R, HEADS * G * J, D), BF16),
        in_specs=[smem, vmem, vmem],
        out_specs=vmem,
        scratch_shapes=[pltpu.VMEM((MESSAGE, D), F32)],
        name="combine",
    )(resp_lengths, jnp.asarray(order.T, BF16), partial.reshape(SPREAD, HEADS, G, ROWS, D))


def solution(mesh):
    names = ("zz", "zc", "y", "xh", "xl", "c")
    fine = Mesh(mesh.devices.reshape(ZZ, ZC, Y, XH, XL, C), names)
    ctx, head = names[:4], names[4:]
    return jax.shard_map(
        per_device,
        mesh=fine,
        in_specs=(
            P(ctx, head, None),
            P(ctx, head, None),
            P(ctx),
            P(ctx + head, None, None, None),
            P(ctx + head, None, None, None),
            P(ctx + head, None, None, None),
            P(),
            P(),
        ),
        out_specs=P(ctx + head, None, None, None),
        check_vma=False,
    )
```

```python
import functools
import math

import jax
import jax.numpy as jnp
import numpy as np
from jax import lax
from jax.experimental import pallas as pl
from jax.experimental.pallas import tpu as pltpu
from jax.sharding import Mesh, PartitionSpec as P

ZZ, ZC, Y, XH, XL, C = 4, 2, 4, 2, 2, 2
HEADS = XL * C
SPREAD = ZZ * ZC
PLANE = SPREAD * HEADS
HOLD = Y * XH
T, R, G, J, D = 2, 2, 2, 5, 128
LIVE = R * T * J
ROWS = 24
BLOCK = 256
QUERIES = T * R * HEADS * G * J
MESSAGE = HEADS * G * ROWS
MASK = 4 * BLOCK
OWN = MASK + 16
OWN_ROWS = HEADS * R * T
PACK = OWN + 2 * G * OWN_ROWS
OWN_PART = 2 * G * R * T
BLOCKS = ((0, 0), (3, 0), (1, 0), (2, 0), (0, 1), (3, 1), (1, 1), (2, 1))
SOURCES = 16
TILE = SOURCES * ROWS
TILES = PLANE // SOURCES
LOWEST = -1e30
HIDE_FLOPS = int(6 * (1 << 30))
FIRST_FLOPS = int(1 * (1 << 30))
EARLY = 5
LOG2E = math.log2(math.e)
F32 = jnp.float32
BF16 = jnp.bfloat16
CONTRACT_LAST = (((1,), (1,)), ((), ()))


def three_parts(x):
    hi = x.astype(BF16).astype(F32)
    mid = (x - hi).astype(BF16).astype(F32)
    lo = (x - hi - mid).astype(BF16).astype(F32)
    return hi, mid, lo


def device_of(zz, zc, y, xh, head):
    return (((zz * ZC + zc) * Y + y) * XH + xh) * HEADS + head


def place_of(offset):
    dy, dxh = offset
    y = lax.rem(lax.axis_index("y") + dy, Y)
    xh = lax.rem(lax.axis_index("xh") + dxh, XH)
    return device_of(lax.axis_index("zz"), lax.axis_index("zc"), y, xh, 0) // HEADS * BLOCK


def row_parts():
    lane = lax.broadcasted_iota(jnp.int32, (1, TILE), 1)
    source = (lane * 2731) >> 16
    return source, lane - source * ROWS


def hide_rows(reach_ref, mask, offset):
    lane = lax.broadcasted_iota(jnp.int32, (1, D), 1)
    sub = lax.broadcasted_iota(jnp.int32, (8, D), 0)
    reach = jnp.where(sub == 0, reach_ref[0], reach_ref[1])
    first = place_of(offset)
    parts = []
    for i in range(BLOCK // D):
        seen = (mask[i : i + 1, :] > 0.5) & (first + i * D + lane < reach)
        parts.append(jnp.where(seen, 0.0, LOWEST))
    return jnp.concatenate(parts, axis=1)


def hide_kernel(reach_ref, *refs):
    mask_refs, hide_ref = refs[:-1], refs[-1]
    for b, mask_ref in enumerate(mask_refs):
        hide_ref[b] = hide_rows(reach_ref, mask_ref[...].astype(F32), BLOCKS[b])


def bias_of(hide):
    _, within = row_parts()
    row_r = jnp.where(within >= T * J, 1, 0)
    pick = (lax.broadcasted_iota(jnp.int32, (8, TILE), 0) == row_r).astype(F32).astype(BF16)
    return lax.dot_general(
        hide.astype(BF16), pick, (((0,), (0,)), ((), ())), preferred_element_type=F32
    )


def tile_queries(q_ref, tile, g):
    q = q_ref[tile * SOURCES : (tile + 1) * SOURCES, g].astype(F32)
    return q.reshape(TILE, D).astype(BF16)


def block_scores(q, kv_refs, g, bias_ref):
    scores = []
    for b, kv_ref in enumerate(kv_refs):
        keys = kv_ref[g * 2 * BLOCK : g * 2 * BLOCK + BLOCK, :]
        s = lax.dot_general(keys, q, CONTRACT_LAST, preferred_element_type=F32)
        scores.append(s + bias_ref[b])
    return scores


def block_values(kv_refs, g):
    return [kv_ref[g * 2 * BLOCK + BLOCK : (g + 1) * 2 * BLOCK, :] for kv_ref in kv_refs]


def weigh(scores, values, top):
    scale = LOG2E / math.sqrt(D)
    total, summed = 0.0, 0.0
    top = top * scale
    for s, v in zip(scores, values):
        p = jnp.exp2(s * scale - top)
        total = total + jnp.sum(p, axis=0, keepdims=True)
        summed = summed + lax.dot_general(
            v, p.astype(BF16), (((0,), (0,)), ((), ())), preferred_element_type=F32
        )
    return total, summed


def top_of(scores):
    wide = functools.reduce(jnp.maximum, scores)
    return jnp.max(wide, axis=0, keepdims=True)


def finish(outs, lse, tile, out_ref):
    source, within = row_parts()
    mine = lax.broadcasted_iota(jnp.int32, (SOURCES, TILE), 0) == source
    row = lax.broadcasted_iota(jnp.int32, (SOURCES, ROWS, D), 1).reshape(TILE, D)
    lane = lax.broadcasted_iota(jnp.int32, (TILE, D), 1)
    spread = ((row == lane) & (row < LIVE)).astype(F32).astype(BF16)
    stats = 0.0
    for g in range(G):
        for i, part in enumerate(three_parts(lse[g])):
            rows = jnp.where(mine, part, 0.0).astype(BF16)
            rows = jnp.dot(rows, spread, preferred_element_type=F32)
            at = (g * 3 + i) * LIVE
            stats = stats + (pltpu.roll(rows, at, 1) if at else rows)
    at = slice(tile * SOURCES, (tile + 1) * SOURCES)
    spare = lax.broadcasted_iota(jnp.int32, (SOURCES, ROWS, D), 1) == LIVE
    out_ref[at, 0] = jnp.where(spare, stats[:, None, :], outs[0]).astype(BF16)
    out_ref[at, 1] = outs[1].astype(BF16)


def own_seen(tile):
    source, within = row_parts()
    is_r1 = within >= T * J
    in_r = jnp.where(is_r1, within - T * J, within)
    row_r = jnp.where(is_r1, 1, 0)
    row_t = jnp.where(in_r >= J, 1, 0)
    k = lax.broadcasted_iota(jnp.int32, (HOLD * OWN_ROWS, 1), 0)
    own_place = T * ((k >> 2) & 3) + (k & 1)
    for b, offset in enumerate(BLOCKS):
        first = place_of(offset) // BLOCK * HEADS * T
        own_place = own_place + jnp.where((k >> 4) == b, first, 0)
    own_r = (k >> 1) & 1
    zz, zc, y, xh = (lax.axis_index(name) for name in ("zz", "zc", "y", "xh"))
    from_source = tile * SOURCES + source
    row_device = device_of(from_source >> 3, (from_source >> 2) & 1, y, xh, from_source & 3)
    row_place = T * row_device + row_t
    return (own_r == row_r) & (own_place <= row_place)


def own_part(kv_refs, kind):
    at = OWN + kind * OWN_ROWS
    return jnp.concatenate([ref[at : at + OWN_ROWS, :] for ref in kv_refs], axis=0)


def first_kernel(hide_ref, q_ref, *refs):
    kv_refs, (acc_ref, stat_ref, bias_ref) = refs[:EARLY], refs[EARLY:]
    for b in range(EARLY):
        bias_ref[b] = bias_of(hide_ref[b])
    for g in range(G):
        for tile in range(TILES):
            q = tile_queries(q_ref, tile, g)
            scores = block_scores(q, kv_refs, g, bias_ref)
            top = top_of(scores)
            total, summed = weigh(scores, block_values(kv_refs, g), top)
            acc_ref[tile, g] = summed
            stat_ref[tile, g, 0:1, :] = top
            stat_ref[tile, g, 1:2, :] = total


def second_kernel(reach_ref, q_ref, *refs):
    all_refs, (acc_ref, stat_ref, out_ref, bias_ref) = refs[:HOLD], refs[HOLD:]
    kv_refs = all_refs[EARLY:]
    for b, kv_ref in enumerate(kv_refs):
        mask = kv_ref[MASK:OWN, :].astype(F32)
        bias_ref[b] = bias_of(hide_rows(reach_ref, mask, BLOCKS[EARLY + b]))
    own_keys = [own_part(all_refs, g) for g in range(G)]
    own_values = [own_part(all_refs, G + g) for g in range(G)]
    scale = LOG2E / math.sqrt(D)
    for tile in range(TILES):
        seen = own_seen(tile)
        outs, lse = [], []
        for g in range(G):
            q = tile_queries(q_ref, tile, g)
            scores = block_scores(q, kv_refs, g, bias_ref)
            so = lax.dot_general(own_keys[g], q, CONTRACT_LAST, preferred_element_type=F32)
            so = jnp.where(seen, so, LOWEST)
            before = stat_ref[tile, g]
            top_before, total_before = before[0:1, :], before[1:2, :]
            top = jnp.maximum(top_of(scores), jnp.max(so, axis=0, keepdims=True))
            top = jnp.maximum(top, top_before)
            values = block_values(kv_refs, g) + [own_values[g]]
            total, summed = weigh(scores + [so], values, top)
            shrink = jnp.exp2((top_before - top) * scale)
            total = total + total_before * shrink
            summed = (summed + acc_ref[tile, g] * shrink) * (1.0 / total)
            outs.append(jnp.transpose(summed).reshape(SOURCES, ROWS, D))
            lse.append(top * scale + jnp.log2(total))
        finish(outs, lse, tile, out_ref)


def combine_kernel(lengths_ref, order_ref, in_ref, out_ref, rows_ref):
    lane = lax.broadcasted_iota(jnp.int32, (1, ROWS, D), 2)
    row = lax.broadcasted_iota(jnp.int32, (1, ROWS, D), 1)
    for h in range(HEADS):
        parts = [in_ref[:, h, g].astype(F32) for g in range(G)]
        stats = parts[0][:, LIVE : LIVE + 1, :]
        for g in range(G):
            mine = False
            for i in range(3):
                mine = mine | (lane == (g * 3 + i) * LIVE + row)
            mine = mine & (row < LIVE)
            lse = jnp.sum(jnp.where(mine, stats, 0.0), axis=2, keepdims=True)
            top = jnp.max(lse, axis=0, keepdims=True)
            w = jnp.exp2(lse - top)
            o = jnp.sum(parts[g] * w, axis=0) / jnp.sum(w, axis=0)
            at = (h * G + g) * ROWS
            rows_ref[at : at + ROWS, :] = jnp.where(row[0] < LIVE, o, 0.0)
    rows = jnp.dot(order_ref[...], rows_ref[...].astype(BF16), preferred_element_type=F32)
    heads = HEADS * G * J
    names = ("zz", "zc", "y", "xh")
    head = lax.axis_index("xl") * C + lax.axis_index("c")
    first = T * device_of(*(lax.axis_index(name) for name in names), head)
    for t in range(T):
        for r in range(R):
            at = (t * R + r) * heads
            live = first + t < lengths_ref[r]
            out_ref[t, r] = jnp.where(live, rows[at : at + heads, :], 0.0).astype(BF16)


def message_order():
    order = np.zeros((MESSAGE, QUERIES), np.float32)
    for h in range(HEADS):
        for g in range(G):
            for r in range(R):
                for t in range(T):
                    for j in range(J):
                        to = (h * G + g) * ROWS + (r * T + t) * J + j
                        order[to, (t * R + r) * HEADS * G * J + (h * G + g) * J + j] = 1
    return order


def own_order():
    kv_heads = HEADS * G
    order = np.zeros((2 * T * R * kv_heads, 2 * T * R * kv_heads), np.float32)
    for h in range(HEADS):
        for kv in range(2):
            for g in range(G):
                for r in range(R):
                    for t in range(T):
                        to = ((h * 2 + kv) * G + g) * R * T + r * T + t
                        order[to, (kv * T * R + t * R + r) * kv_heads + h * G + g] = 1
    return order


def own_kernel(own_order_ref, k_ref, v_ref, *refs):
    own_refs, own_rows = refs[:HEADS], refs[HEADS]
    own = [ref[...].astype(F32).reshape(T * R * HEADS * G, D) for ref in (k_ref, v_ref)]
    own = jnp.concatenate(own, axis=0).astype(BF16)
    own = jnp.dot(own_order_ref[...], own, preferred_element_type=F32)
    own_rows[...] = own.reshape(HEADS, OWN_PART, D)
    head = lax.axis_index("xl") * C + lax.axis_index("c")
    for step, own_ref in enumerate(own_refs):
        own_ref[...] = own_rows[lax.rem(head + step, HEADS)].astype(BF16)


def message_kernel(order_ref, q_ref, message_ref):
    q = q_ref[...].astype(F32).reshape(QUERIES, D).astype(BF16)
    rows = jnp.dot(order_ref[...], q, preferred_element_type=F32).astype(BF16)
    for to in range(SPREAD):
        message_ref[to] = rows


def pack_kernel(mask_ref, k_ref, v_ref, *refs):
    own_refs, (pack_ref, wide, by_head, sorted_rows) = refs[:HEADS], refs[HEADS:]
    for kv, ref in enumerate((k_ref, v_ref)):
        wide[kv] = ref[...].astype(F32)
        for g in range(G):
            at = (g * 2 + kv) * BLOCK
            pack_ref[at : at + BLOCK, :] = wide[kv, pl.ds(g, BLOCK, stride=G), :].astype(BF16)
    head = lax.axis_index("xl") * C + lax.axis_index("c")
    for step, own_ref in enumerate(own_refs):
        by_head[lax.rem(head + HEADS - step, HEADS)] = own_ref[...].astype(F32)
    part = T * R
    for h in range(HEADS):
        for kind in range(2 * G):
            at = kind * OWN_ROWS + h * part
            sorted_rows[at : at + part, :] = by_head[h, kind * part : (kind + 1) * part, :]
    pack_ref[OWN:PACK, :] = sorted_rows[...].astype(BF16)
    by_head[0] = jnp.zeros((OWN_PART, D), F32)
    by_head[0, 0 : BLOCK // D, :] = mask_ref[...].astype(F32)
    pack_ref[MASK:OWN, :] = by_head[0].astype(BF16)


def permute(x, axis, size, shift):
    return lax.ppermute(x, axis, [(i, (i + shift) % size) for i in range(size)])


def per_device(
    prompt_keys,
    prompt_values,
    prompt_mask,
    response_queries,
    response_keys,
    response_values,
    resp_lengths,
    prompt_reach,
):
    plane = ("zz", "zc", "xl", "c")
    smem = pl.BlockSpec(memory_space=pltpu.SMEM)
    vmem = pl.BlockSpec(memory_space=pltpu.VMEM)
    order = message_order()
    own = pl.pallas_call(
        own_kernel,
        out_shape=[jax.ShapeDtypeStruct((OWN_PART, D), BF16)] * HEADS,
        in_specs=[vmem] * 3,
        out_specs=[vmem] * HEADS,
        scratch_shapes=[pltpu.VMEM((HEADS, OWN_PART, D), F32)],
        name="own",
    )(jnp.asarray(own_order(), BF16), response_keys, response_values)
    own = [own[0]] + [permute(own[step], ("xl", "c"), HEADS, step) for step in range(1, HEADS)]
    message = pl.pallas_call(
        message_kernel,
        out_shape=jax.ShapeDtypeStruct((SPREAD, MESSAGE, D), BF16),
        in_specs=[vmem] * 2,
        out_specs=vmem,
        name="message",
    )(jnp.asarray(order, BF16), response_queries)
    kv = pl.pallas_call(
        pack_kernel,
        out_shape=jax.ShapeDtypeStruct((PACK, D), BF16),
        in_specs=[vmem] * (3 + HEADS),
        out_specs=vmem,
        scratch_shapes=[
            pltpu.VMEM((2, G * BLOCK, D), F32),
            pltpu.VMEM((HEADS, OWN_PART, D), F32),
            pltpu.VMEM((HEADS * OWN_PART, D), F32),
        ],
        compiler_params=pltpu.CompilerParams(vmem_limit_bytes=6 << 20),
        name="pack",
    )(
        prompt_mask.reshape(BLOCK // D, D),
        prompt_keys.reshape(BLOCK * G, D),
        prompt_values.reshape(BLOCK * G, D),
        *own,
    )
    message, kv = lax.optimization_barrier((message, kv))
    across = permute(kv, "xh", XH, 1)
    far = permute(kv, "y", Y, 2)
    before = permute(kv, "y", Y, 1)
    after = permute(kv, "y", Y, 3)
    rows = lax.all_to_all(message.reshape(PLANE, G * ROWS, D), plane, 0, 0, tiled=True)
    across_before = permute(across, "y", Y, 1)
    across_after = permute(across, "y", Y, 3)
    across_far = permute(far, "xh", XH, 1)
    blocks = (kv, before, after, far, across, across_before, across_after, across_far)
    hide = pl.pallas_call(
        hide_kernel,
        out_shape=jax.ShapeDtypeStruct((EARLY, 8, BLOCK), F32),
        grid=(1,),
        in_specs=[smem]
        + [pl.BlockSpec((OWN - MASK, D), lambda i: (MASK // 16, 0))] * (EARLY),
        out_specs=pl.BlockSpec((EARLY, 8, BLOCK), lambda i: (0, 0, 0)),
        compiler_params=pltpu.CompilerParams(vmem_limit_bytes=4 << 20),
        cost_estimate=pl.CostEstimate(flops=HIDE_FLOPS, bytes_accessed=1 << 20, transcendentals=0),
        name="hide",
    )(prompt_reach, *blocks[:EARLY])
    rows = rows.reshape(PLANE, G, ROWS, D)
    acc, stat = pl.pallas_call(
        first_kernel,
        out_shape=[
            jax.ShapeDtypeStruct((TILES, G, D, TILE), F32),
            jax.ShapeDtypeStruct((TILES, G, 8, TILE), F32),
        ],
        in_specs=[vmem] * (2 + EARLY),
        out_specs=[vmem] * 2,
        scratch_shapes=[pltpu.VMEM((EARLY, BLOCK, TILE), F32)],
        compiler_params=pltpu.CompilerParams(vmem_limit_bytes=24 << 20),
        cost_estimate=pl.CostEstimate(flops=FIRST_FLOPS, bytes_accessed=2 << 20, transcendentals=0),
        name="attend_first",
    )(hide, rows, *blocks[:EARLY])
    partial = pl.pallas_call(
        second_kernel,
        out_shape=jax.ShapeDtypeStruct((PLANE, G, ROWS, D), BF16),
        in_specs=[smem] + [vmem] * (3 + HOLD),
        out_specs=vmem,
        scratch_shapes=[pltpu.VMEM((HOLD - EARLY, BLOCK, TILE), F32)],
        compiler_params=pltpu.CompilerParams(vmem_limit_bytes=24 << 20),
        cost_estimate=pl.CostEstimate(flops=2 << 30, bytes_accessed=3 << 20, transcendentals=0),
        name="attend_second",
    )(prompt_reach, rows, *blocks, acc, stat)
    partial = lax.all_to_all(partial.reshape(PLANE, G * ROWS, D), plane, 0, 0, tiled=True)
    return pl.pallas_call(
        combine_kernel,
        out_shape=jax.ShapeDtypeStruct((T, R, HEADS * G * J, D), BF16),
        in_specs=[smem, vmem, vmem],
        out_specs=vmem,
        scratch_shapes=[pltpu.VMEM((MESSAGE, D), F32)],
        compiler_params=pltpu.CompilerParams(vmem_limit_bytes=6 << 20),
        name="combine",
    )(resp_lengths, jnp.asarray(order.T, BF16), partial.reshape(SPREAD, HEADS, G, ROWS, D))


def solution(mesh):
    names = ("zz", "zc", "y", "xh", "xl", "c")
    fine = Mesh(mesh.devices.reshape(ZZ, ZC, Y, XH, XL, C), names)
    ctx, head = names[:4], names[4:]
    return jax.shard_map(
        per_device,
        mesh=fine,
        in_specs=(
            P(ctx, head, None),
            P(ctx, head, None),
            P(ctx),
            P(ctx + head, None, None, None),
            P(ctx + head, None, None, None),
            P(ctx + head, None, None, None),
            P(),
            P(),
        ),
        out_specs=P(ctx + head, None, None, None),
        check_vma=False,
    )
```

```python
import functools
import math

import jax
import jax.numpy as jnp
import numpy as np
from jax import lax
from jax.experimental import pallas as pl
from jax.experimental.pallas import tpu as pltpu
from jax.sharding import Mesh, PartitionSpec as P

ZZ, ZC, Y, XH, XL, C = 4, 2, 4, 2, 2, 2
HEADS = XL * C
SPREAD = ZZ * ZC
PLANE = SPREAD * HEADS
HOLD = Y * XH
T, R, G, J, D = 2, 2, 2, 5, 128
LIVE = R * T * J
ROWS = 24
BLOCK = 256
QUERIES = T * R * HEADS * G * J
MESSAGE = HEADS * G * ROWS
MASK = 4 * BLOCK
OWN = MASK + 16
OWN_ROWS = HEADS * R * T
PACK = OWN + 2 * G * OWN_ROWS
OWN_PART = 2 * G * R * T
BLOCKS = ((0, 0), (3, 0), (1, 0), (2, 0), (0, 1), (3, 1), (1, 1), (2, 1))
SOURCES = 16
TILE = SOURCES * ROWS
TILES = PLANE // SOURCES
LOWEST = -1e30
HIDE_FLOPS = int(6 * (1 << 30))
FIRST_FLOPS = int(1 * (1 << 30))
EARLY = 5
LOG2E = math.log2(math.e)
F32 = jnp.float32
BF16 = jnp.bfloat16
CONTRACT_LAST = (((1,), (1,)), ((), ()))


def three_parts(x):
    hi = x.astype(BF16).astype(F32)
    mid = (x - hi).astype(BF16).astype(F32)
    lo = (x - hi - mid).astype(BF16).astype(F32)
    return hi, mid, lo


def device_of(zz, zc, y, xh, head):
    return (((zz * ZC + zc) * Y + y) * XH + xh) * HEADS + head


def place_of(offset):
    dy, dxh = offset
    y = lax.rem(lax.axis_index("y") + dy, Y)
    xh = lax.rem(lax.axis_index("xh") + dxh, XH)
    return device_of(lax.axis_index("zz"), lax.axis_index("zc"), y, xh, 0) // HEADS * BLOCK


def row_parts():
    lane = lax.broadcasted_iota(jnp.int32, (1, TILE), 1)
    source = (lane * 2731) >> 16
    return source, lane - source * ROWS


def hide_rows(reach_ref, mask, offset):
    lane = lax.broadcasted_iota(jnp.int32, (1, D), 1)
    sub = lax.broadcasted_iota(jnp.int32, (8, D), 0)
    reach = jnp.where(sub == 0, reach_ref[0], reach_ref[1])
    first = place_of(offset)
    parts = []
    for i in range(BLOCK // D):
        seen = (mask[i : i + 1, :] > 0.5) & (first + i * D + lane < reach)
        parts.append(jnp.where(seen, 0.0, LOWEST))
    return jnp.concatenate(parts, axis=1)


def hide_kernel(reach_ref, lengths_ref, *refs):
    mask_refs, (hide_ref, live_ref) = refs[:-2], refs[-2:]
    names = ("zz", "zc", "y", "xh")
    head = lax.axis_index("xl") * C + lax.axis_index("c")
    first = T * device_of(*(lax.axis_index(name) for name in names), head)
    for t in range(T):
        for r in range(R):
            at = (t * R + r) * HEADS * G * J
            live = jnp.where(first + t < lengths_ref[r], 1.0, 0.0)
            live_ref[at : at + HEADS * G * J, :] = jnp.full((HEADS * G * J, D), live, F32)
    for b, mask_ref in enumerate(mask_refs):
        hide_ref[b] = hide_rows(reach_ref, mask_ref[...].astype(F32), BLOCKS[b])


def bias_of(hide):
    _, within = row_parts()
    row_r = jnp.where(within >= T * J, 1, 0)
    pick = (lax.broadcasted_iota(jnp.int32, (8, TILE), 0) == row_r).astype(F32).astype(BF16)
    return lax.dot_general(
        hide.astype(BF16), pick, (((0,), (0,)), ((), ())), preferred_element_type=F32
    )


def tile_queries(q_ref, tile, g):
    q = q_ref[tile * SOURCES : (tile + 1) * SOURCES, g].astype(F32)
    return q.reshape(TILE, D).astype(BF16)


def block_scores(q, kv_refs, g, bias_ref):
    scores = []
    for b, kv_ref in enumerate(kv_refs):
        keys = kv_ref[g * 2 * BLOCK : g * 2 * BLOCK + BLOCK, :]
        s = lax.dot_general(keys, q, CONTRACT_LAST, preferred_element_type=F32)
        scores.append(s + bias_ref[b])
    return scores


def block_values(kv_refs, g):
    return [kv_ref[g * 2 * BLOCK + BLOCK : (g + 1) * 2 * BLOCK, :] for kv_ref in kv_refs]


def weigh(scores, values, top):
    scale = LOG2E / math.sqrt(D)
    total, summed = 0.0, 0.0
    top = top * scale
    for s, v in zip(scores, values):
        p = jnp.exp2(s * scale - top)
        total = total + jnp.sum(p, axis=0, keepdims=True)
        summed = summed + lax.dot_general(
            v, p.astype(BF16), (((0,), (0,)), ((), ())), preferred_element_type=F32
        )
    return total, summed


def top_of(scores):
    wide = functools.reduce(jnp.maximum, scores)
    return jnp.max(wide, axis=0, keepdims=True)


def finish(outs, lse, tile, out_ref):
    source, within = row_parts()
    mine = lax.broadcasted_iota(jnp.int32, (SOURCES, TILE), 0) == source
    row = lax.broadcasted_iota(jnp.int32, (SOURCES, ROWS, D), 1).reshape(TILE, D)
    lane = lax.broadcasted_iota(jnp.int32, (TILE, D), 1)
    spread = ((row == lane) & (row < LIVE)).astype(F32).astype(BF16)
    stats = 0.0
    for g in range(G):
        for i, part in enumerate(three_parts(lse[g])):
            rows = jnp.where(mine, part, 0.0).astype(BF16)
            rows = jnp.dot(rows, spread, preferred_element_type=F32)
            at = (g * 3 + i) * LIVE
            stats = stats + (pltpu.roll(rows, at, 1) if at else rows)
    at = slice(tile * SOURCES, (tile + 1) * SOURCES)
    spare = lax.broadcasted_iota(jnp.int32, (SOURCES, ROWS, D), 1) == LIVE
    out_ref[at, 0] = jnp.where(spare, stats[:, None, :], outs[0]).astype(BF16)
    out_ref[at, 1] = outs[1].astype(BF16)


def own_seen(tile):
    source, within = row_parts()
    is_r1 = within >= T * J
    in_r = jnp.where(is_r1, within - T * J, within)
    row_r = jnp.where(is_r1, 1, 0)
    row_t = jnp.where(in_r >= J, 1, 0)
    k = lax.broadcasted_iota(jnp.int32, (HOLD * OWN_ROWS, 1), 0)
    own_place = T * ((k >> 2) & 3) + (k & 1)
    for b, offset in enumerate(BLOCKS):
        first = place_of(offset) // BLOCK * HEADS * T
        own_place = own_place + jnp.where((k >> 4) == b, first, 0)
    own_r = (k >> 1) & 1
    zz, zc, y, xh = (lax.axis_index(name) for name in ("zz", "zc", "y", "xh"))
    from_source = tile * SOURCES + source
    row_device = device_of(from_source >> 3, (from_source >> 2) & 1, y, xh, from_source & 3)
    row_place = T * row_device + row_t
    return (own_r == row_r) & (own_place <= row_place)


def own_part(kv_refs, kind):
    at = OWN + kind * OWN_ROWS
    return jnp.concatenate([ref[at : at + OWN_ROWS, :] for ref in kv_refs], axis=0)


def first_kernel(hide_ref, q_ref, *refs):
    kv_refs, (acc_ref, stat_ref, bias_ref) = refs[:EARLY], refs[EARLY:]
    for b in range(EARLY):
        bias_ref[b] = bias_of(hide_ref[b])
    for g in range(G):
        for tile in range(TILES):
            q = tile_queries(q_ref, tile, g)
            scores = block_scores(q, kv_refs, g, bias_ref)
            top = top_of(scores)
            total, summed = weigh(scores, block_values(kv_refs, g), top)
            acc_ref[tile, g] = summed
            stat_ref[tile, g, 0:1, :] = top
            stat_ref[tile, g, 1:2, :] = total


def second_kernel(reach_ref, q_ref, *refs):
    all_refs, (acc_ref, stat_ref, out_ref, bias_ref) = refs[:HOLD], refs[HOLD:]
    kv_refs = all_refs[EARLY:]
    for b, kv_ref in enumerate(kv_refs):
        mask = kv_ref[MASK:OWN, :].astype(F32)
        bias_ref[b] = bias_of(hide_rows(reach_ref, mask, BLOCKS[EARLY + b]))
    own_keys = [own_part(all_refs, g) for g in range(G)]
    own_values = [own_part(all_refs, G + g) for g in range(G)]
    scale = LOG2E / math.sqrt(D)
    for tile in range(TILES):
        seen = own_seen(tile)
        outs, lse = [], []
        for g in range(G):
            q = tile_queries(q_ref, tile, g)
            scores = block_scores(q, kv_refs, g, bias_ref)
            so = lax.dot_general(own_keys[g], q, CONTRACT_LAST, preferred_element_type=F32)
            so = jnp.where(seen, so, LOWEST)
            before = stat_ref[tile, g]
            top_before, total_before = before[0:1, :], before[1:2, :]
            top = jnp.maximum(top_of(scores), jnp.max(so, axis=0, keepdims=True))
            top = jnp.maximum(top, top_before)
            values = block_values(kv_refs, g) + [own_values[g]]
            total, summed = weigh(scores + [so], values, top)
            shrink = jnp.exp2((top_before - top) * scale)
            total = total + total_before * shrink
            summed = (summed + acc_ref[tile, g] * shrink) * (1.0 / total)
            outs.append(jnp.transpose(summed).reshape(SOURCES, ROWS, D))
            lse.append(top * scale + jnp.log2(total))
        finish(outs, lse, tile, out_ref)


def combine_kernel(live_ref, order_ref, in_ref, out_ref, rows_ref):
    lane = lax.broadcasted_iota(jnp.int32, (1, ROWS, D), 2)
    row = lax.broadcasted_iota(jnp.int32, (1, ROWS, D), 1)
    for h in range(HEADS):
        parts = [in_ref[:, h, g].astype(F32) for g in range(G)]
        stats = parts[0][:, LIVE : LIVE + 1, :]
        for g in range(G):
            mine = False
            for i in range(3):
                mine = mine | (lane == (g * 3 + i) * LIVE + row)
            mine = mine & (row < LIVE)
            lse = jnp.sum(jnp.where(mine, stats, 0.0), axis=2, keepdims=True)
            top = jnp.max(lse, axis=0, keepdims=True)
            w = jnp.exp2(lse - top)
            o = jnp.sum(parts[g] * w, axis=0) / jnp.sum(w, axis=0)
            at = (h * G + g) * ROWS
            rows_ref[at : at + ROWS, :] = jnp.where(row[0] < LIVE, o, 0.0)
    rows = jnp.dot(order_ref[...], rows_ref[...].astype(BF16), preferred_element_type=F32)
    heads = HEADS * G * J
    for t in range(T):
        for r in range(R):
            at = (t * R + r) * heads
            live = live_ref[at : at + heads, :] > 0.5
            out_ref[t, r] = jnp.where(live, rows[at : at + heads, :], 0.0).astype(BF16)


def message_order():
    order = np.zeros((MESSAGE, QUERIES), np.float32)
    for h in range(HEADS):
        for g in range(G):
            for r in range(R):
                for t in range(T):
                    for j in range(J):
                        to = (h * G + g) * ROWS + (r * T + t) * J + j
                        order[to, (t * R + r) * HEADS * G * J + (h * G + g) * J + j] = 1
    return order


def own_order():
    kv_heads = HEADS * G
    order = np.zeros((2 * T * R * kv_heads, 2 * T * R * kv_heads), np.float32)
    for h in range(HEADS):
        for kv in range(2):
            for g in range(G):
                for r in range(R):
                    for t in range(T):
                        to = ((h * 2 + kv) * G + g) * R * T + r * T + t
                        order[to, (kv * T * R + t * R + r) * kv_heads + h * G + g] = 1
    return order


def own_kernel(own_order_ref, k_ref, v_ref, *refs):
    own_refs, own_rows = refs[:HEADS], refs[HEADS]
    own = [ref[...].astype(F32).reshape(T * R * HEADS * G, D) for ref in (k_ref, v_ref)]
    own = jnp.concatenate(own, axis=0).astype(BF16)
    own = jnp.dot(own_order_ref[...], own, preferred_element_type=F32)
    own_rows[...] = own.reshape(HEADS, OWN_PART, D)
    head = lax.axis_index("xl") * C + lax.axis_index("c")
    for step, own_ref in enumerate(own_refs):
        own_ref[...] = own_rows[lax.rem(head + step, HEADS)].astype(BF16)


def message_kernel(order_ref, q_ref, message_ref):
    q = q_ref[...].astype(F32).reshape(QUERIES, D).astype(BF16)
    rows = jnp.dot(order_ref[...], q, preferred_element_type=F32).astype(BF16)
    for to in range(SPREAD):
        message_ref[to] = rows


def pack_kernel(mask_ref, k_ref, v_ref, *refs):
    own_refs, (pack_ref, wide, by_head, sorted_rows) = refs[:HEADS], refs[HEADS:]
    for kv, ref in enumerate((k_ref, v_ref)):
        wide[kv] = ref[...].astype(F32)
        for g in range(G):
            at = (g * 2 + kv) * BLOCK
            pack_ref[at : at + BLOCK, :] = wide[kv, pl.ds(g, BLOCK, stride=G), :].astype(BF16)
    head = lax.axis_index("xl") * C + lax.axis_index("c")
    for step, own_ref in enumerate(own_refs):
        by_head[lax.rem(head + HEADS - step, HEADS)] = own_ref[...].astype(F32)
    part = T * R
    for h in range(HEADS):
        for kind in range(2 * G):
            at = kind * OWN_ROWS + h * part
            sorted_rows[at : at + part, :] = by_head[h, kind * part : (kind + 1) * part, :]
    pack_ref[OWN:PACK, :] = sorted_rows[...].astype(BF16)
    by_head[0] = jnp.zeros((OWN_PART, D), F32)
    by_head[0, 0 : BLOCK // D, :] = mask_ref[...].astype(F32)
    pack_ref[MASK:OWN, :] = by_head[0].astype(BF16)


def permute(x, axis, size, shift):
    return lax.ppermute(x, axis, [(i, (i + shift) % size) for i in range(size)])


def per_device(
    prompt_keys,
    prompt_values,
    prompt_mask,
    response_queries,
    response_keys,
    response_values,
    resp_lengths,
    prompt_reach,
):
    plane = ("zz", "zc", "xl", "c")
    smem = pl.BlockSpec(memory_space=pltpu.SMEM)
    vmem = pl.BlockSpec(memory_space=pltpu.VMEM)
    order = message_order()
    own = pl.pallas_call(
        own_kernel,
        out_shape=[jax.ShapeDtypeStruct((OWN_PART, D), BF16)] * HEADS,
        in_specs=[vmem] * 3,
        out_specs=[vmem] * HEADS,
        scratch_shapes=[pltpu.VMEM((HEADS, OWN_PART, D), F32)],
        name="own",
    )(jnp.asarray(own_order(), BF16), response_keys, response_values)
    own = [own[0]] + [permute(own[step], ("xl", "c"), HEADS, step) for step in range(1, HEADS)]
    message = pl.pallas_call(
        message_kernel,
        out_shape=jax.ShapeDtypeStruct((SPREAD, MESSAGE, D), BF16),
        in_specs=[vmem] * 2,
        out_specs=vmem,
        name="message",
    )(jnp.asarray(order, BF16), response_queries)
    kv = pl.pallas_call(
        pack_kernel,
        out_shape=jax.ShapeDtypeStruct((PACK, D), BF16),
        in_specs=[vmem] * (3 + HEADS),
        out_specs=vmem,
        scratch_shapes=[
            pltpu.VMEM((2, G * BLOCK, D), F32),
            pltpu.VMEM((HEADS, OWN_PART, D), F32),
            pltpu.VMEM((HEADS * OWN_PART, D), F32),
        ],
        compiler_params=pltpu.CompilerParams(vmem_limit_bytes=6 << 20),
        name="pack",
    )(
        prompt_mask.reshape(BLOCK // D, D),
        prompt_keys.reshape(BLOCK * G, D),
        prompt_values.reshape(BLOCK * G, D),
        *own,
    )
    message, kv = lax.optimization_barrier((message, kv))
    across = permute(kv, "xh", XH, 1)
    far = permute(kv, "y", Y, 2)
    before = permute(kv, "y", Y, 1)
    after = permute(kv, "y", Y, 3)
    rows = lax.all_to_all(message.reshape(PLANE, G * ROWS, D), plane, 0, 0, tiled=True)
    across_before = permute(across, "y", Y, 1)
    across_after = permute(across, "y", Y, 3)
    across_far = permute(far, "xh", XH, 1)
    blocks = (kv, before, after, far, across, across_before, across_after, across_far)
    hide, live = pl.pallas_call(
        hide_kernel,
        out_shape=[
            jax.ShapeDtypeStruct((EARLY, 8, BLOCK), F32),
            jax.ShapeDtypeStruct((QUERIES, D), F32),
        ],
        grid=(1,),
        in_specs=[smem] * 2
        + [pl.BlockSpec((OWN - MASK, D), lambda i: (MASK // 16, 0))] * (EARLY),
        out_specs=[
            pl.BlockSpec((EARLY, 8, BLOCK), lambda i: (0, 0, 0)),
            pl.BlockSpec((QUERIES, D), lambda i: (0, 0)),
        ],
        compiler_params=pltpu.CompilerParams(vmem_limit_bytes=4 << 20),
        cost_estimate=pl.CostEstimate(flops=HIDE_FLOPS, bytes_accessed=1 << 20, transcendentals=0),
        name="hide",
    )(prompt_reach, resp_lengths, *blocks[:EARLY])
    rows = rows.reshape(PLANE, G, ROWS, D)
    acc, stat = pl.pallas_call(
        first_kernel,
        out_shape=[
            jax.ShapeDtypeStruct((TILES, G, D, TILE), F32),
            jax.ShapeDtypeStruct((TILES, G, 8, TILE), F32),
        ],
        in_specs=[vmem] * (2 + EARLY),
        out_specs=[vmem] * 2,
        scratch_shapes=[pltpu.VMEM((EARLY, BLOCK, TILE), F32)],
        compiler_params=pltpu.CompilerParams(vmem_limit_bytes=24 << 20),
        cost_estimate=pl.CostEstimate(flops=FIRST_FLOPS, bytes_accessed=2 << 20, transcendentals=0),
        name="attend_first",
    )(hide, rows, *blocks[:EARLY])
    partial = pl.pallas_call(
        second_kernel,
        out_shape=jax.ShapeDtypeStruct((PLANE, G, ROWS, D), BF16),
        in_specs=[smem] + [vmem] * (3 + HOLD),
        out_specs=vmem,
        scratch_shapes=[pltpu.VMEM((HOLD - EARLY, BLOCK, TILE), F32)],
        compiler_params=pltpu.CompilerParams(vmem_limit_bytes=24 << 20),
        cost_estimate=pl.CostEstimate(flops=2 << 30, bytes_accessed=3 << 20, transcendentals=0),
        name="attend_second",
    )(prompt_reach, rows, *blocks, acc, stat)
    partial = lax.all_to_all(partial.reshape(PLANE, G * ROWS, D), plane, 0, 0, tiled=True)
    return pl.pallas_call(
        combine_kernel,
        out_shape=jax.ShapeDtypeStruct((T, R, HEADS * G * J, D), BF16),
        in_specs=[vmem] * 3,
        out_specs=vmem,
        scratch_shapes=[pltpu.VMEM((MESSAGE, D), F32)],
        compiler_params=pltpu.CompilerParams(vmem_limit_bytes=6 << 20),
        name="combine",
    )(live, jnp.asarray(order.T, BF16), partial.reshape(SPREAD, HEADS, G, ROWS, D))


def solution(mesh):
    names = ("zz", "zc", "y", "xh", "xl", "c")
    fine = Mesh(mesh.devices.reshape(ZZ, ZC, Y, XH, XL, C), names)
    ctx, head = names[:4], names[4:]
    return jax.shard_map(
        per_device,
        mesh=fine,
        in_specs=(
            P(ctx, head, None),
            P(ctx, head, None),
            P(ctx),
            P(ctx + head, None, None, None),
            P(ctx + head, None, None, None),
            P(ctx + head, None, None, None),
            P(),
            P(),
        ),
        out_specs=P(ctx + head, None, None, None),
        check_vma=False,
    )
```
